128 devices in a mesh: ctx: 32 (over x, z, core), own: 4 (over y).
Axes of the slice: x: 4, y: 4, z: 4, core: 2. Of those that a mesh axis runs over, the one named last changes fastest.
Arguments:
- query_proj: bfloat16 [16384, 8192], P(('ctx', 'own')), may hold values from -6 to 6
- key_proj: bfloat16 [16384, 8192], P(('ctx', 'own')), may hold values from -6 to 6
- value_proj: bfloat16 [16384, 8192], P(('ctx', 'own')), may hold values from -6 to 6
- short_taps: float32 [3, 7, 512], P(None, None, 'own'), may hold values from -2 to 2
- long_taps: float32 [128, 512], P(None, 'own'), may hold values from -0.5 to 0.5
- decay_rate: float32 [8, 8192], P(None, 'own'), may hold values from 3.0517579e-06 to 0.03
- residues: float32 [8, 8192], P(None, 'own'), may hold values from -2 to 2
- grad_out: bfloat16 [16384, 8192], P(('ctx', 'own')), may hold values from -6 to 6
Outputs:
- layer_out: bfloat16 [16384, 8192], P(('ctx', 'own'))
- grad_query: bfloat16 [16384, 8192], P(('ctx', 'own'))
- grad_key: bfloat16 [16384, 8192], P(('ctx', 'own'))
- grad_value: bfloat16 [16384, 8192], P(('ctx', 'own'))
- grad_long_taps: float32 [128, 512], P(None, 'own')
The draws below stay inside these ranges and needn't reach their ends.
All inputs are finite; a program needn't handle non-finite values.
Results may differ from the reference program's by a relative error of at most 0.02.
Values may be sent and summed in bfloat16 or wider, within the bound.
No kernel may reach another device: no remote copies, remote signals or barrier semaphores. Data moves between devices by JAX's collectives and lax.ppermute only.
A program may use at most 256 MiB of HBM per device.

```python
import math
import jax
import jax.numpy as jnp
from jax import lax

D = 8192
ORDER = 8
SHORT = 7
TAPS = 128
CPG = 16
G = 512
TOKENS = 16384


def shard_levels(key, shape, shards, low, top_value):
    def one(position, parts):
        heights = jax.random.uniform(jax.random.fold_in(jax.random.fold_in(key, 6), position), (parts,), jnp.float32, low / len(shards), top_value / len(shards))
        return jnp.repeat(jnp.exp(heights), shape[position] // parts).reshape((-1,) + (1,) * (len(shape) - position - 1))

    level = one(*shards[0])
    for cut in shards[1:]:
        level = level * one(*cut)
    return level


def bell_draw(stream_key, dims, spread, most, split=(), held_as=jnp.bfloat16):
    result = spread * jax.random.normal(stream_key, dims, jnp.float32)
    if split:
        result = result * shard_levels(stream_key, dims, split, -0.22, 0.18)
    return jnp.clip(result, -most, most).astype(held_as)


def setup_inputs(seed: int = 0) -> dict:
    seeds = jax.random.split(jax.random.key(seed), 9)
    return {
        "query_proj": bell_draw(seeds[0], (TOKENS, D), 1.0, 6.0, ((0, 128),)),
        "key_proj": bell_draw(seeds[1], (TOKENS, D), 1.0, 6.0, ((0, 128),)),
        "value_proj": bell_draw(seeds[2], (TOKENS, D), 1.0, 6.0, ((0, 128),)),
        "short_taps": bell_draw(seeds[3], (3, SHORT, G), SHORT ** -0.5, 2.0, ((2, 4),), jnp.float32),
        "long_taps": bell_draw(seeds[4], (TAPS, G), TAPS ** -0.5, 0.5, ((1, 4),), jnp.float32),
        "decay_rate": jnp.clip(jnp.exp(math.log(0.03) - 9.1932349 * jax.random.uniform(seeds[5], (ORDER, D), jnp.float32) ** shard_levels(seeds[5], (ORDER, D), ((1, 4),), -0.2, 0.2)), 3.051757857974735e-06, 0.03),
        "residues": bell_draw(seeds[6], (ORDER, D), ORDER ** -0.5, 2.0, ((1, 4),), jnp.float32),
        "grad_out": bell_draw(seeds[7], (TOKENS, D), 1.0, 6.0, ((0, 128),)),
    }


def causal_short(rows_in, taps_chan):
    values = rows_in.astype(jnp.float32)
    row_count, chan_count = values.shape
    summed = jnp.zeros((row_count, chan_count), jnp.float32)
    for offset in range(SHORT):
        moved = jnp.concatenate([jnp.zeros((offset, chan_count), jnp.float32), values[:row_count - offset]], axis=0)
        summed = summed + taps_chan[offset][None, :] * moved
    return summed.astype(jnp.bfloat16)

def later_short(rows_in, taps_chan):
    values = rows_in.astype(jnp.float32)
    row_count, chan_count = values.shape
    summed = jnp.zeros((row_count, chan_count), jnp.float32)
    for offset in range(SHORT):
        moved = jnp.concatenate([values[offset:], jnp.zeros((offset, chan_count), jnp.float32)], axis=0)
        summed = summed + taps_chan[offset][None, :] * moved
    return summed.astype(jnp.bfloat16)

def one_block(query, key_rows, value_rows, grad_rows, short_part, taps_part, decay, resid):
    chan_short = jnp.repeat(short_part, CPG, axis=2)
    query_feat = causal_short(query, chan_short[0])
    key_feat = causal_short(key_rows, chan_short[1])
    value_feat = causal_short(value_rows, chan_short[2])
    product = (key_feat.astype(jnp.float32) * value_feat.astype(jnp.float32)).astype(jnp.bfloat16)
    positions = jnp.arange(TOKENS).astype(jnp.float32)
    weight = resid * jnp.sqrt(-jnp.expm1(-2.0 * decay))

    def add_mode(summed, mode):
        return (summed + mode[0][None, :] * jnp.exp(-mode[1][None, :] * positions[:, None]), None)
    start_value = jnp.zeros((TOKENS, decay.shape[1]), jnp.float32)
    filter_full, _ = lax.scan(add_mode, start_value, (weight, decay))
    filter_full = filter_full + jnp.pad(jnp.repeat(taps_part, CPG, axis=1), ((0, TOKENS - TAPS), (0, 0)))
    fft_size = 2 * TOKENS
    filter_spec = jnp.fft.rfft(filter_full, n=fft_size, axis=0)
    product_spec = jnp.fft.rfft(product.astype(jnp.float32), n=fft_size, axis=0)
    long_conv = jnp.fft.irfft(product_spec * filter_spec, n=fft_size, axis=0)[:TOKENS]
    grad_float = grad_rows.astype(jnp.float32)
    layer_out = (query_feat.astype(jnp.float32) * long_conv).astype(jnp.bfloat16)
    grad_conv = (grad_float * query_feat.astype(jnp.float32)).astype(jnp.bfloat16)
    grad_qfeat = (grad_float * long_conv).astype(jnp.bfloat16)
    conv_spec = jnp.fft.rfft(grad_conv.astype(jnp.float32), n=fft_size, axis=0)
    grad_prod = jnp.fft.irfft(conv_spec * jnp.conj(filter_spec), n=fft_size, axis=0)[:TOKENS]
    grad_kfeat = (grad_prod * value_feat.astype(jnp.float32)).astype(jnp.bfloat16)
    grad_vfeat = (grad_prod * key_feat.astype(jnp.float32)).astype(jnp.bfloat16)
    grad_query = later_short(grad_qfeat, chan_short[0])
    grad_key = later_short(grad_kfeat, chan_short[1])
    grad_value = later_short(grad_vfeat, chan_short[2])
    correlation = jnp.fft.irfft(conv_spec * jnp.conj(product_spec), n=fft_size, axis=0)[:TAPS]
    group_count = correlation.shape[1] // CPG
    grad_taps = correlation.reshape(TAPS, group_count, CPG).sum(axis=2) / math.sqrt(TOKENS * CPG)
    return (layer_out, grad_query, grad_key, grad_value, grad_taps)

def reference(query_proj, key_proj, value_proj, short_taps, long_taps, decay_rate, residues, grad_out):
    groups = D // CPG
    block_groups = math.gcd(groups, 16)
    block_chan = block_groups * CPG

    def one_step(block_index, outputs):
        first_chan = (block_index * block_chan).astype(jnp.int32)
        first_group = (block_index * block_groups).astype(jnp.int32)

        def chan_slice(array):
            return lax.dynamic_slice_in_dim(array, first_chan, block_chan, array.ndim - 1)

        def group_slice(array):
            return lax.dynamic_slice_in_dim(array, first_group, block_groups, array.ndim - 1)
        results = one_block(chan_slice(query_proj), chan_slice(key_proj), chan_slice(value_proj), chan_slice(grad_out), group_slice(short_taps), group_slice(long_taps), chan_slice(decay_rate), chan_slice(residues))
        updated = []
        for position_out in range(4):
            updated.append(lax.dynamic_update_slice_in_dim(outputs[position_out], results[position_out], first_chan, 1))
        updated.append(lax.dynamic_update_slice_in_dim(outputs[4], results[4], first_group, 1))
        return tuple(updated)
    initial = (jnp.zeros((TOKENS, D), jnp.bfloat16), jnp.zeros((TOKENS, D), jnp.bfloat16), jnp.zeros((TOKENS, D), jnp.bfloat16), jnp.zeros((TOKENS, D), jnp.bfloat16), jnp.zeros((TAPS, groups), jnp.float32))
    layer_out, grad_query, grad_key, grad_value, grad_taps = lax.fori_loop(0, groups // block_groups, one_step, initial)
    return (layer_out, grad_query, grad_key, grad_value, grad_taps)
```

```python
import math

import jax
import jax.numpy as jnp
import numpy as np
from jax import lax
from jax.experimental import pallas as pl
from jax.experimental.pallas import tpu as pltpu
from jax.sharding import PartitionSpec as P

CPG = 16
BLOCK = 512
TERMS = 16
RATE_TOP = 0.03
AXES = ("ctx", "own")
F32, BF16 = jnp.float32, jnp.bfloat16


def split_np(table):
    high = table.astype(np.float32).astype(jnp.bfloat16)
    low = (table - high.astype(np.float64)).astype(np.float32).astype(jnp.bfloat16)
    return high, low


def series(lags):
    nodes = np.cos(np.pi * (np.arange(64) + 0.5) / 64)
    values = np.exp(-np.outer(np.asarray(lags, np.float64), RATE_TOP / 2 * (1 + nodes)))
    basis = np.cos(np.outer(np.arange(TERMS), np.pi * (np.arange(64) + 0.5) / 64))
    coeff = values @ basis.T * (2.0 / 64)
    coeff[:, 0] *= 0.5
    return coeff


def tables(rows):
    angle = np.pi * (2 * np.arange(rows) + 1) / (2 * rows)

    def forward(places):
        phase = np.outer(angle, places)
        return np.concatenate([np.cos(phase), -np.sin(phase)])

    here = np.arange(rows)
    own, before, after = forward(here), forward(here - rows), forward(here + rows)
    phase = np.outer(here, angle)
    inverse = np.concatenate([np.cos(phase), -np.sin(phase)], axis=1) / rows
    cat = np.concatenate
    pair = lambda m: cat(split_np(m), axis=1)

    def triple(m):
        high, low = split_np(m)
        return cat([high, low, high], axis=1)

    return dict(
        own=pair(own),
        before=pair(before),
        after=pair(after),
        taps=triple(own),
        head=triple(own @ series(here)),
        inverse=split_np(inverse)[0],
        inverse3=triple(inverse),
        ahead=triple(series(here + 1)),
        behind=triple(series(rows - here)),
        moment=cat(
            [
                pair(series(rows - 1 - here).T),
                pair(series(here).T),
            ],
            axis=0,
        ),
    )


def dot(a, b):
    return jnp.dot(a, b, preferred_element_type=F32)


def halves(x):
    high = x.astype(BF16)
    return high, (x - high.astype(F32)).astype(BF16)


def stack3(x):
    high, low = halves(x)
    return jnp.concatenate([high, high, low], axis=0)


def spread_matrix(groups, quarter, copies=1):
    row = lax.broadcasted_iota(jnp.int32, (copies * groups, BLOCK), 0) % groups
    col = lax.broadcasted_iota(jnp.int32, (copies * groups, BLOCK), 1)
    return (row == col // CPG + quarter * (BLOCK // CPG)).astype(F32).astype(BF16)


def spread_taps(short, quarter, out):
    high, rest = halves(short)
    rest = short - high.astype(F32)
    mid, rest2 = halves(rest)
    low = rest2
    lhs = jnp.concatenate([high, mid, low], axis=1)
    out[...] = dot(lhs, spread_matrix(128, quarter, 3))


def chebyshev(rate):
    z = rate * (2.0 / RATE_TOP) - 1.0
    terms = [jnp.ones_like(z), z]
    while len(terms) < TERMS:
        terms.append(2.0 * z * terms[-1] - terms[-2])
    return terms


def front_kernel(
    me, q, k, v, g, rim, short, rates, moment,
    qf, kf, vf, prod, gconv, sf, sb, xq, xk, xv, taps,
):
    rows = q.shape[0]
    quarter = pl.program_id(0)
    spread_taps(short[0], quarter, taps)
    for at, (src, dst) in enumerate(((q, xq), (k, xk), (v, xv))):
        dst[0:8] = rim[8 * at : 8 * at + 8].astype(F32)
        dst[8:] = src[...].astype(F32)

    def step(r, _):
        base = pl.multiple_of(r * 16, 16)
        feats = []
        for at, src in enumerate((xq, xk, xv)):
            window = src[pl.ds(base, 24), :]
            total = taps[7 * at : 7 * at + 1, :] * window[8:24]
            for j in range(1, 7):
                total = total + taps[7 * at + j : 7 * at + j + 1, :] * window[8 - j : 24 - j]
            feats.append(total.astype(BF16))
        here = pl.ds(base, 16)
        qf[here, :] = feats[0]
        kf[here, :] = feats[1]
        vf[here, :] = feats[2]
        prod[here, :] = (feats[1].astype(F32) * feats[2].astype(F32)).astype(BF16)
        gconv[here, :] = (g[here, :].astype(F32) * feats[0].astype(F32)).astype(BF16)
        return 0

    lax.fori_loop(0, rows // 16, step, 0)
    p, c = prod[...], gconv[...]
    mf = dot(moment[0:16, :], jnp.concatenate([p, p], axis=0))
    mb = dot(moment[16:32, :], jnp.concatenate([c, c], axis=0))
    for lane in range(BLOCK // 128):
        cols = slice(128 * lane, 128 * lane + 128)
        terms = chebyshev(rates[0, 8 * lane : 8 * lane + 8, :])
        ahead = jnp.zeros((8, 128), F32)
        back = jnp.zeros((8, 128), F32)
        for n, term in enumerate(terms):
            ahead = ahead + term * mf[n : n + 1, cols]
            back = back + term * mb[n : n + 1, cols]
        sf[lane] = ahead.astype(BF16)
        sb[lane] = back.astype(BF16)


def scan_kernel(me, states, rates, out):
    count = states.shape[0]
    backward = me[1]
    factor = jnp.exp(rates[0] * -128.0)

    def hop(n, carry):
        at = jnp.where(backward == 1, count - 1 - n, n)
        out[at] = carry.astype(BF16)
        return factor * carry + states[at].astype(F32)

    lax.fori_loop(0, count, hop, jnp.zeros((8, 128), F32), unroll=4)


def back_kernel(
    me, qf, kf, vf, g, prod, gconv, before, after, sf, sb, short, rates, weights, ltaps,
    t_own, t_before, t_after, t_taps, t_head, t_inv, t_inv3, t_ahead, t_behind, *rest,
):
    outs = rest[-27:]
    (layer, gq, gk, gv, rim, last, tgrad) = outs[:7]
    (xx, own, prv, cur, nxt, tre, hre, ys, zs, cs, tsp, acc, taps, eq, ek, ev, coef, lg, gp, _unused) = outs[7:]
    rows = qf.shape[0]
    quarter = pl.program_id(0)
    spread_taps(short[0], quarter, taps)

    @pl.when(quarter == 0)
    def _():
        spec = dot(t_taps[...], stack3(ltaps[0]))
        high, low = halves(spec)
        tsp[:, 0:128] = high
        tsp[:, 128:256] = low
        acc[...] = jnp.zeros_like(acc)

    tre[...] = dot(tsp[...], spread_matrix(128, quarter, 2))
    for src, table, dst in (
        (prod, t_own, own), (before, t_before, prv), (gconv, t_own, cur), (after, t_after, nxt),
    ):
        value = src[...]
        xx[0:rows] = value
        xx[rows:] = value
        dst[...] = dot(table[...], xx[...])
    for lane in range(BLOCK // 128):
        cols = slice(128 * lane, 128 * lane + 128)
        eight = slice(8 * lane, 8 * lane + 8)
        weight = weights[0, eight, :]
        sets = (weight, weight * sf[lane].astype(F32), weight * sb[lane].astype(F32))
        for n, term in enumerate(chebyshev(rates[0, eight, :])):
            for at, field in enumerate(sets):
                coef[16 * at + n : 16 * at + n + 1, cols] = jnp.sum(
                    term * field, axis=0, keepdims=True
                )
    hre[...] = dot(t_head[...], stack3(coef[0:16]))

    def bins(r, _):
        base = pl.multiple_of(r * 16, 16)
        re = pl.ds(base, 16)
        im = pl.ds(rows + base, 16)
        for lane in range(BLOCK // 128):
            cols = slice(128 * lane, 128 * lane + 128)
            tr, ti, hr, hi = tre[re, cols], tre[im, cols], hre[re, cols], hre[im, cols]
            pr, pi, cr, ci = own[re, cols], own[im, cols], cur[re, cols], cur[im, cols]
            wr, wi = pr + prv[re, cols], pi + prv[im, cols]
            ar, ai = cr + nxt[re, cols], ci + nxt[im, cols]
            ys[re, cols] = (wr * tr - wi * ti + (pr * hr - pi * hi)).astype(BF16)
            ys[im, cols] = (wr * ti + wi * tr + (pr * hi + pi * hr)).astype(BF16)
            zs[re, cols] = (ar * tr + ai * ti + (cr * hr + ci * hi)).astype(BF16)
            zs[im, cols] = (ai * tr - ar * ti + (ci * hr - cr * hi)).astype(BF16)
            cs[re, cols] = (cr * wr + ci * wi).astype(BF16)
            cs[im, cols] = (ci * wr - cr * wi).astype(BF16)
        return 0

    lax.fori_loop(0, rows // 16, bins, 0)
    lg[...] = dot(t_inv[...], ys[...]) + dot(t_ahead[...], stack3(coef[16:32]))
    gp[...] = dot(t_inv[...], zs[...]) + dot(t_behind[...], stack3(coef[32:48]))
    chan = lax.broadcasted_iota(jnp.int32, (BLOCK, 128), 0)
    group = lax.broadcasted_iota(jnp.int32, (BLOCK, 128), 1)
    gather = (chan // CPG + quarter * (BLOCK // CPG) == group).astype(F32).astype(BF16)
    acc[...] += dot(cs[...], gather)

    @pl.when(quarter == pl.num_programs(0) - 1)
    def _():
        tgrad[...] = dot(t_inv3[...], stack3(acc[...]))

    def rows_out(r, _):
        here = pl.ds(pl.multiple_of(r * 16, 16), 16)
        conv, grad = lg[here, :], gp[here, :]
        layer[here, :] = (qf[here, :].astype(F32) * conv).astype(BF16)
        eq[here, :] = (g[here, :].astype(F32) * conv).astype(BF16).astype(F32)
        ek[here, :] = (grad * vf[here, :].astype(F32)).astype(BF16).astype(F32)
        ev[here, :] = (grad * kf[here, :].astype(F32)).astype(BF16).astype(F32)
        return 0

    lax.fori_loop(0, rows // 16, rows_out, 0)
    for at, src in enumerate((eq, ek, ev)):
        src[rows:] = jnp.zeros((8, BLOCK), F32)
        rim[8 * at : 8 * at + 8] = src[0:8].astype(BF16)

    def unfeature(r):
        base = r * 16 if isinstance(r, int) else pl.multiple_of(r * 16, 16)
        sums = []
        for at, src in enumerate((eq, ek, ev)):
            window = src[pl.ds(base, 24), :]
            total = taps[7 * at : 7 * at + 1, :] * window[0:16]
            for j in range(1, 7):
                total = total + taps[7 * at + j : 7 * at + j + 1, :] * window[j : 16 + j]
            sums.append(total)
        return sums

    def finish(r, _):
        here = pl.ds(pl.multiple_of(r * 16, 16), 16)
        for dst, total in zip((gq, gk, gv), unfeature(r)):
            dst[here, :] = total.astype(BF16)
        return 0

    lax.fori_loop(0, rows // 16, finish, 0)
    for at, total in enumerate(unfeature(rows // 16 - 1)):
        last[16 * at : 16 * at + 16] = total


def tail_kernel(me, last, rim, short, gq_in, gk_in, gv_in, gq, gk, gv, taps):
    quarter = pl.program_id(0) % 4
    spread_taps(short[0], quarter, taps)
    for at, dst in enumerate((gq, gk, gv)):
        window = jnp.concatenate(
            [jnp.zeros((16, BLOCK), F32), rim[8 * at : 8 * at + 8].astype(F32)], axis=0
        )
        total = last[16 * at : 16 * at + 16]
        for j in range(1, 7):
            total = total + taps[7 * at + j : 7 * at + j + 1, :] * window[j : 16 + j]
        dst[...] = total.astype(BF16)


def shift(value, steps):
    count = lax.axis_size(AXES)
    first, last = max(0, -steps), min(count, count - steps)
    return lax.ppermute(value, AXES, [(at, at + steps) for at in range(first, last)])


def gather_own(value):
    count = lax.axis_size("own")
    parts = [value]
    for hop in range(1, count):
        parts.append(lax.ppermute(value, "own", [(at, (at + hop) % count) for at in range(count)]))
    return jnp.stack(parts)


def tiles(x):
    rows, width = x.shape
    return x.reshape(rows, width // 128, 128).transpose(1, 0, 2).reshape(-1, 128)


def params_of(vmem):
    return pltpu.CompilerParams(
        dimension_semantics=("arbitrary",), vmem_limit_bytes=vmem
    )


def shards(query, key, value, short_taps, long_taps, decay_rate, residues, grad_out):
    rows, width = query.shape
    owners = lax.axis_size("own")
    per_own = width // owners
    steps = per_own // BLOCK
    ctx, own = lax.axis_index("ctx"), lax.axis_index("own")
    flat = ctx * owners + own
    half = width // 128
    me = jnp.stack([own, flat // half, flat % half]).astype(jnp.int32)
    table = tables(rows)

    short = jnp.pad(short_taps.reshape(-1, short_taps.shape[2]), ((0, 3), (0, 0)))
    short_all = gather_own(short)
    rims = shift(jnp.concatenate([query[rows - 8 :], key[rows - 8 :], value[rows - 8 :]]), 1)
    weight = residues * jnp.sqrt(-jnp.expm1(-2.0 * decay_rate))
    poles_all = gather_own(jnp.concatenate([tiles(decay_rate), tiles(weight), long_taps]))

    def slot(me_ref, chunk):
        return (me_ref[0] - chunk) % owners

    tab = lambda name: (jnp.asarray(table[name]), pl.BlockSpec(table[name].shape, lambda i, m: (0, 0)))
    full = jax.ShapeDtypeStruct((rows, width), BF16)
    part = jax.ShapeDtypeStruct((rows, per_own), BF16)
    state = jax.ShapeDtypeStruct((per_own // 128, 8, 128), BF16)
    group = BLOCK // 128

    def front(chunk):
        wide = pl.BlockSpec((rows, BLOCK), lambda i, m: (0, chunk * steps + i))
        here = pl.BlockSpec((rows, BLOCK), lambda i, m: (0, i))
        sspec = pl.BlockSpec((group, 8, 128), lambda i, m: (i, 0, 0))
        moment, moment_spec = tab("moment")
        return pl.pallas_call(
            front_kernel,
            out_shape=(part,) * 5 + (state,) * 2,
            grid_spec=pltpu.PrefetchScalarGridSpec(
                num_scalar_prefetch=1,
                grid=(steps,),
                in_specs=[wide] * 4
                + [
                    pl.BlockSpec((24, BLOCK), lambda i, m: (0, chunk * steps + i)),
                    pl.BlockSpec((1, 24, 128), lambda i, m: (slot(m, chunk), 0, 0)),
                    pl.BlockSpec((1, 8 * group, 128), lambda i, m: (slot(m, chunk), i, 0)),
                    moment_spec,
                ],
                out_specs=(here,) * 5 + (sspec,) * 2,
                scratch_shapes=[pltpu.VMEM((rows + 8, BLOCK), F32)] * 3
                + [pltpu.VMEM((24, BLOCK), F32)],
            ),
            compiler_params=params_of(32 << 20),
            cost_estimate=pl.CostEstimate(
                flops=2_000_000_000, transcendentals=0, bytes_accessed=10_000_000
            ),
            name=f"front{chunk}",
        )(me, query, key, value, grad_out, rims, short_all, poles_all, moment)

    fronts, behinds, aheads = [], [], []
    for chunk in range(owners):
        made = front(chunk)
        fronts.append(made)
        behinds.append(shift(made[3], 1))
        aheads.append(shift(made[4], -1))

    states = jnp.concatenate([f[5] for f in fronts] + [f[6] for f in fronts])
    arrived = lax.all_to_all(states, AXES, 0, 0, tiled=True)
    scanned = pl.pallas_call(
        scan_kernel,
        out_shape=jax.ShapeDtypeStruct(arrived.shape, BF16),
        grid_spec=pltpu.PrefetchScalarGridSpec(
            num_scalar_prefetch=1,
            grid=(1,),
            in_specs=[
                pl.BlockSpec(arrived.shape, lambda i, m: (0, 0, 0)),
                pl.BlockSpec(
                    (1, 8, 128),
                    lambda i, m: ((m[0] - m[2] // (half // owners)) % owners, m[2] % (half // owners), 0),
                ),
            ],
            out_specs=pl.BlockSpec(arrived.shape, lambda i, m: (0, 0, 0)),
        ),
        compiler_params=params_of(16 << 20),
        name="scan",
    )(me, arrived, poles_all)
    carried = lax.all_to_all(scanned, AXES, 0, 0, tiled=True)

    names = ("own", "before", "after", "taps", "head", "inverse", "inverse3", "ahead", "behind")

    def back(chunk, outs):
        wide = pl.BlockSpec((rows, BLOCK), lambda i, m: (0, chunk * steps + i))
        here = pl.BlockSpec((rows, BLOCK), lambda i, m: (0, i))
        quarter = per_own // 128
        consts = [tab(name) for name in names]
        made = fronts[chunk]
        operands = [
            me, made[0], made[1], made[2], grad_out, made[3], made[4],
            behinds[chunk], aheads[chunk], carried, carried, short_all,
            poles_all, poles_all, poles_all,
        ] + [c for c, _ in consts]
        blocks = quarter // group
        in_specs = [
            here, here, here, wide, here, here, here, here,
            pl.BlockSpec((group, 8, 128), lambda i, m: (chunk * blocks + i, 0, 0)),
            pl.BlockSpec((group, 8, 128), lambda i, m: ((owners + chunk) * blocks + i, 0, 0)),
            pl.BlockSpec((1, 24, 128), lambda i, m: (slot(m, chunk), 0, 0)),
            pl.BlockSpec((1, 8 * group, 128), lambda i, m: (slot(m, chunk), i, 0)),
            pl.BlockSpec((1, 8 * group, 128), lambda i, m: (slot(m, chunk), blocks + i, 0)),
            pl.BlockSpec((1, 128, 128), lambda i, m: (slot(m, chunk), 2, 0)),
        ] + [s for _, s in consts]
        aliases = {}
        for at, out in enumerate(outs):
            aliases[len(operands)] = at
            operands.append(out)
            in_specs.append(pl.BlockSpec(memory_space=pl.ANY))
        spectrum = pltpu.VMEM((2 * rows, BLOCK), F32)
        packed = pltpu.VMEM((2 * rows, BLOCK), BF16)
        ext = pltpu.VMEM((rows + 8, BLOCK), F32)
        plain = pltpu.VMEM((rows, BLOCK), F32)
        return pl.pallas_call(
            back_kernel,
            out_shape=(full,) * 4
            + (
                jax.ShapeDtypeStruct((24, per_own), BF16),
                jax.ShapeDtypeStruct((48, per_own), F32),
                jax.ShapeDtypeStruct((128, 128), F32),
            ),
            grid_spec=pltpu.PrefetchScalarGridSpec(
                num_scalar_prefetch=1,
                grid=(steps,),
                in_specs=in_specs,
                out_specs=(wide,) * 4
                + (
                    pl.BlockSpec((24, BLOCK), lambda i, m: (0, i)),
                    pl.BlockSpec((48, BLOCK), lambda i, m: (0, i)),
                    pl.BlockSpec((128, 128), lambda i, m: (0, 0)),
                ),
                scratch_shapes=[packed]
                + [spectrum] * 6
                + [packed] * 3
                + [
                    pltpu.VMEM((2 * rows, 256), BF16),
                    pltpu.VMEM((2 * rows, 128), F32),
                    pltpu.VMEM((24, BLOCK), F32),
                    ext, ext, ext,
                    pltpu.VMEM((48, BLOCK), F32),
                    plain, plain,
                    pltpu.VMEM((8, 128), F32),
                ],
            ),
            input_output_aliases=aliases,
            compiler_params=params_of(48 << 20),
            cost_estimate=pl.CostEstimate(
                flops=4_000_000_000, transcendentals=0, bytes_accessed=16_000_000
            ),
            name=f"back{chunk}",
        )(*operands)

    outs, edges, lasts, partial = (), [], [], []
    for chunk in range(owners):
        made = back(chunk, outs)
        outs = made[:4]
        edges.append(shift(made[4], -1))
        lasts.append(made[5])
        partial.append(made[6])

    def tail(chunk, outs):
        strip = pl.BlockSpec((16, BLOCK), lambda i, m: (rows // 16 - 1, chunk * steps + i))
        anyspec = pl.BlockSpec(memory_space=pl.ANY)
        thin = jax.ShapeDtypeStruct((rows, width), BF16)
        return pl.pallas_call(
            tail_kernel,
            out_shape=(thin,) * 3,
            grid_spec=pltpu.PrefetchScalarGridSpec(
                num_scalar_prefetch=1,
                grid=(steps,),
                in_specs=[
                    pl.BlockSpec((48, BLOCK), lambda i, m: (0, i)),
                    pl.BlockSpec((24, BLOCK), lambda i, m: (0, i)),
                    pl.BlockSpec((1, 24, 128), lambda i, m: (slot(m, chunk), 0, 0)),
                    anyspec, anyspec, anyspec,
                ],
                out_specs=(strip,) * 3,
                scratch_shapes=[pltpu.VMEM((24, BLOCK), F32)],
            ),
            input_output_aliases={4: 0, 5: 1, 6: 2},
            compiler_params=params_of(16 << 20),
            name=f"tail{chunk}",
        )(me, lasts[chunk], edges[chunk], short_all, *outs)

    grads = outs[1:4]
    for chunk in range(owners):
        grads = tail(chunk, grads)

    ctxs = lax.axis_size("ctx")
    share = rows // ctxs
    pieces = jnp.stack([p.reshape(ctxs, share, 128) for p in partial], axis=1)
    landed = lax.all_to_all(pieces.reshape(ctxs * owners, share, 128), AXES, 0, 0, tiled=True)
    tokens = rows * ctxs * owners
    total = landed.sum(axis=0) * (1.0 / math.sqrt(tokens * CPG))
    every = lax.all_to_all(
        jnp.broadcast_to(total[None], (ctxs, share, 128)), "ctx", 0, 0, tiled=True
    )
    return (outs[0],) + tuple(grads) + (every.reshape(rows, 128),)


def solution(mesh):
    placed = (
        P(AXES, None),
        P(AXES, None),
        P(AXES, None),
        P(None, None, "own"),
        P(None, "own"),
        P(None, "own"),
        P(None, "own"),
        P(AXES, None),
    )
    return jax.shard_map(
        shards,
        mesh=mesh,
        in_specs=placed,
        out_specs=(P(AXES, None),) * 4 + (P(None, "own"),),
        check_vma=False,
    )
```

```python
import math

import jax
import jax.numpy as jnp
import numpy as np
from jax import lax
from jax.experimental import pallas as pl
from jax.experimental.pallas import tpu as pltpu
from jax.sharding import PartitionSpec as P

CPG = 16
BLOCK = 512
CHUNKS = 2
TERMS = 16
RATE_TOP = 0.03
AXES = ("ctx", "own")
F32, BF16 = jnp.float32, jnp.bfloat16


def split_np(table):
    high = table.astype(np.float32).astype(jnp.bfloat16)
    low = (table - high.astype(np.float64)).astype(np.float32).astype(jnp.bfloat16)
    return high, low


def series(lags):
    nodes = np.cos(np.pi * (np.arange(64) + 0.5) / 64)
    values = np.exp(-np.outer(np.asarray(lags, np.float64), RATE_TOP / 2 * (1 + nodes)))
    basis = np.cos(np.outer(np.arange(TERMS), np.pi * (np.arange(64) + 0.5) / 64))
    coeff = values @ basis.T * (2.0 / 64)
    coeff[:, 0] *= 0.5
    return coeff


def tables(rows):
    angle = np.pi * (2 * np.arange(rows) + 1) / (2 * rows)

    def forward(places):
        phase = np.outer(angle, places)
        return np.concatenate([np.cos(phase), -np.sin(phase)])

    here = np.arange(rows)
    own, before, after = forward(here), forward(here - rows), forward(here + rows)
    phase = np.outer(here, angle)
    inverse = np.concatenate([np.cos(phase), -np.sin(phase)], axis=1) / rows
    cat = np.concatenate
    pair = lambda m: cat(split_np(m), axis=1)

    def triple(m):
        high, low = split_np(m)
        return cat([high, low, high], axis=1)

    return dict(
        own=pair(own),
        before=pair(before),
        after=pair(after),
        taps=triple(own),
        head=triple(own @ series(here)),
        inverse=split_np(inverse)[0],
        inverse3=triple(inverse),
        ahead=triple(series(here + 1)),
        behind=triple(series(rows - here)),
        spread=(np.arange(16 * rows)[None, :] // CPG == here[:, None]).astype(jnp.bfloat16),
        moment=cat(
            [
                pair(series(rows - 1 - here).T),
                pair(series(here).T),
            ],
            axis=0,
        ),
    )


def dot(a, b):
    return jnp.dot(a, b, preferred_element_type=F32)


def halves(x):
    high = x.astype(BF16)
    return high, (x - high.astype(F32)).astype(BF16)


def stack3(x):
    high, low = halves(x)
    return jnp.concatenate([high, high, low], axis=0)


def spread_taps(short, spread):
    high, _ = halves(short)
    rest = short - high.astype(F32)
    mid, low = halves(rest)
    made = dot(jnp.concatenate([high, mid, low], axis=0), spread)
    return made[0:24] + made[24:48] + made[48:72]


def chebyshev(rate):
    z = rate * (2.0 / RATE_TOP) - 1.0
    terms = [jnp.ones_like(z), z]
    while len(terms) < TERMS:
        terms.append(2.0 * z * terms[-1] - terms[-2])
    return terms


def pack_kernel(q, k, v, short, rate, resid, ltaps, rim, small, big):
    for at, src in enumerate((q, k, v)):
        rim[8 * at : 8 * at + 8] = src[...]
    small[...] = jnp.zeros_like(small)
    for at in range(3):
        small[7 * at : 7 * at + 7] = short[at]
    for tile in range(rate.shape[1] // 128):
        cols = slice(128 * tile, 128 * tile + 128)
        big[8 * tile : 8 * tile + 8] = rate[:, cols]
        big[128 + 8 * tile : 136 + 8 * tile] = resid[:, cols]
    big[256:] = ltaps[...]


def front_kernel(
    me, q, k, v, g, rim, short, moment, spread,
    qf, kf, vf, prod, gconv, mom, taps, xq, xk, xv,
):
    rows = q.shape[0]
    taps[...] = spread_taps(short[0], spread[...])
    lanes = range(BLOCK // 128)
    for at, (src, dst) in enumerate(((q, xq), (k, xk), (v, xv))):
        for lane in lanes:
            cols = slice(128 * lane, 128 * lane + 128)
            dst[lane, 0:8] = rim[8 * at : 8 * at + 8, cols].astype(F32)
            dst[lane, 8:] = src[:, cols].astype(F32)

    def step(r, _):
        base = pl.multiple_of(r * 32, 32)
        here = pl.ds(base, 32)
        for lane in lanes:
            cols = slice(128 * lane, 128 * lane + 128)
            feats = []
            for at, src in enumerate((xq, xk, xv)):
                total = taps[7 * at : 7 * at + 1, cols] * src[lane, pl.ds(base + 8, 32), :]
                for j in range(1, 7):
                    tap = taps[7 * at + j : 7 * at + j + 1, cols]
                    total = total + tap * src[lane, pl.ds(base + 8 - j, 32), :]
                feats.append(total.astype(BF16))
            qf[here, cols] = feats[0]
            kf[here, cols] = feats[1]
            vf[here, cols] = feats[2]
            prod[here, cols] = (feats[1].astype(F32) * feats[2].astype(F32)).astype(BF16)
            gconv[here, cols] = (g[here, cols].astype(F32) * feats[0].astype(F32)).astype(BF16)
        return 0

    lax.fori_loop(0, rows // 32, step, 0)
    p, c = prod[...], gconv[...]
    mom[0:16] = dot(moment[0:16, :], jnp.concatenate([p, p], axis=0))
    mom[16:32] = dot(moment[16:32, :], jnp.concatenate([c, c], axis=0))


def state_kernel(me, *refs):
    moms, rates, out = refs[:CHUNKS], refs[CHUNKS], refs[CHUNKS + 1]
    owners = rates.shape[0]
    per = out.shape[0] // (2 * owners)
    for own in range(owners):
        chunk, part = divmod(own, owners // CHUNKS)
        mom = moms[chunk]
        slot = (me[0] - own + owners) % owners

        def tile(n, _):
            eight = pl.ds(pl.multiple_of(n * 8, 8), 8)
            cols = pl.ds(pl.multiple_of((part * per + n) * 128, 128), 128)
            terms = chebyshev(rates[slot, eight, :])
            mine = mom[:, cols]
            ahead = terms[0] * mine[0:1]
            back = terms[0] * mine[16:17]
            for at in range(1, TERMS):
                ahead = ahead + terms[at] * mine[at : at + 1]
                back = back + terms[at] * mine[16 + at : 17 + at]
            out[own * per + n] = ahead.astype(BF16)
            out[(owners + own) * per + n] = back.astype(BF16)
            return 0

        lax.fori_loop(0, per, tile, 0, unroll=4)


def scan_kernel(me, states, rates, out):
    count = states.shape[0]
    backward = me[1]
    factor = jnp.exp(rates[0] * -128.0)

    def hop(n, carry):
        at = jnp.where(backward == 1, count - 1 - n, n)
        out[at] = carry.astype(BF16)
        return factor * carry + states[at].astype(F32)

    lax.fori_loop(0, count, hop, jnp.zeros((8, 128), F32), unroll=8)


def modal_weight(rate, resid):
    x = 2.0 * rate
    return resid * jnp.sqrt(x * modal_series(x))


def modal_series(x):
    total = 1.0 - x * (1.0 / 8)
    for n in (7, 6, 5, 4, 3, 2):
        total = 1.0 - x * (1.0 / n) * total
    return total


def mid_kernel(
    me, prod, gconv, before, after, rates, resids, ltaps,
    t_own, t_before, t_after, t_taps, t_head, t_inv3, spread,
    yout, zout, tgrad, xx, own, prv, cur, nxt, tre, hre, cs, tsp, acc, coef,
):
    rows = prod.shape[0]
    quarter = pl.program_id(0) % (128 * CPG // BLOCK)

    @pl.when(quarter == 0)
    def _():
        spec = dot(t_taps[...], stack3(ltaps[0]))
        high, low = halves(spec)
        tsp[:, 0:128] = high
        tsp[:, 128:256] = low
        acc[...] = jnp.zeros_like(acc)

    one_hot = spread[...]
    xx[0:128] = one_hot
    xx[128:256] = one_hot
    tre[...] = dot(tsp[...], xx[...])
    for src, table, dst in (
        (prod, t_own, own), (before, t_before, prv), (gconv, t_own, cur), (after, t_after, nxt),
    ):
        value = src[...]
        xx[0:rows] = value
        xx[rows:] = value
        dst[...] = dot(table[...], xx[...])
    for lane in range(BLOCK // 128):
        cols = slice(128 * lane, 128 * lane + 128)
        eight = slice(8 * lane, 8 * lane + 8)
        weight = modal_weight(rates[0, eight, :], resids[0, eight, :])
        for n, term in enumerate(chebyshev(rates[0, eight, :])):
            coef[n : n + 1, cols] = jnp.sum(term * weight, axis=0, keepdims=True)
    hre[...] = dot(t_head[...], stack3(coef[...]))

    def bins(r, _):
        base = pl.multiple_of(r * 16, 16)
        re = pl.ds(base, 16)
        im = pl.ds(rows + base, 16)
        for lane in range(BLOCK // 128):
            cols = slice(128 * lane, 128 * lane + 128)
            tr, ti, hr, hi = tre[re, cols], tre[im, cols], hre[re, cols], hre[im, cols]
            pr, pi, cr, ci = own[re, cols], own[im, cols], cur[re, cols], cur[im, cols]
            wr, wi = pr + prv[re, cols], pi + prv[im, cols]
            ar, ai = cr + nxt[re, cols], ci + nxt[im, cols]
            yout[re, cols] = (wr * tr - wi * ti + (pr * hr - pi * hi)).astype(BF16)
            yout[im, cols] = (wr * ti + wi * tr + (pr * hi + pi * hr)).astype(BF16)
            zout[re, cols] = (ar * tr + ai * ti + (cr * hr + ci * hi)).astype(BF16)
            zout[im, cols] = (ai * tr - ar * ti + (ci * hr - cr * hi)).astype(BF16)
            cs[re, cols] = (cr * wr + ci * wi).astype(BF16)
            cs[im, cols] = (ci * wr - cr * wi).astype(BF16)
        return 0

    lax.fori_loop(0, rows // 16, bins, 0)
    acc[...] += lax.dot_general(
        cs[...], spread[...], (((1,), (1,)), ((), ())), preferred_element_type=F32
    )

    @pl.when(quarter == 128 * CPG // BLOCK - 1)
    def _():
        tgrad[...] = dot(t_inv3[...], stack3(acc[...]))


def back_kernel(
    me, qf, kf, vf, g, ys, zs, sf, sb, taps, rates, resids,
    t_inv, t_ahead, t_behind, *rest,
):
    (layer, gq, gk, gv, rim, last, eq, ek, ev, coef, lg, gp) = rest[-12:]
    rows = qf.shape[0]
    lanes = range(BLOCK // 128)
    for lane in lanes:
        cols = slice(128 * lane, 128 * lane + 128)
        eight = slice(8 * lane, 8 * lane + 8)
        weight = modal_weight(rates[0, eight, :], resids[0, eight, :])
        sets = (weight * sf[lane].astype(F32), weight * sb[lane].astype(F32))
        for n, term in enumerate(chebyshev(rates[0, eight, :])):
            for at, field in enumerate(sets):
                coef[16 * at + n : 16 * at + n + 1, cols] = jnp.sum(
                    term * field, axis=0, keepdims=True
                )
    lg[...] = dot(t_inv[...], ys[...]) + dot(t_ahead[...], stack3(coef[0:16]))
    gp[...] = dot(t_inv[...], zs[...]) + dot(t_behind[...], stack3(coef[16:32]))

    def rows_out(r, _):
        here = pl.ds(pl.multiple_of(r * 16, 16), 16)
        for lane in lanes:
            cols = slice(128 * lane, 128 * lane + 128)
            conv, grad = lg[here, cols], gp[here, cols]
            layer[here, cols] = (qf[here, cols].astype(F32) * conv).astype(BF16)
            eq[lane, here] = (g[here, cols].astype(F32) * conv).astype(BF16).astype(F32)
            ek[lane, here] = (grad * vf[here, cols].astype(F32)).astype(BF16).astype(F32)
            ev[lane, here] = (grad * kf[here, cols].astype(F32)).astype(BF16).astype(F32)
        return 0

    lax.fori_loop(0, rows // 16, rows_out, 0)
    for at, src in enumerate((eq, ek, ev)):
        for lane in lanes:
            cols = slice(128 * lane, 128 * lane + 128)
            src[lane, rows:] = jnp.zeros((8, 128), F32)
            rim[8 * at : 8 * at + 8, cols] = src[lane, 0:8].astype(BF16)

    def finish(r, _):
        base = pl.multiple_of(r * 32, 32)
        here = pl.ds(base, 32)
        for lane in lanes:
            cols = slice(128 * lane, 128 * lane + 128)
            for at, (src, dst) in enumerate(((eq, gq), (ek, gk), (ev, gv))):
                total = taps[7 * at : 7 * at + 1, cols] * src[lane, here, :]
                for j in range(1, 7):
                    tap = taps[7 * at + j : 7 * at + j + 1, cols]
                    total = total + tap * src[lane, pl.ds(base + j, 32), :]
                dst[here, cols] = total.astype(BF16)
                last[8 * at : 8 * at + 8, cols] = total[24:32]
        return 0

    lax.fori_loop(0, rows // 32, finish, 0)


def tail_kernel(me, *refs):
    lasts, rims, taps = refs[:CHUNKS], refs[CHUNKS : 2 * CHUNKS], refs[2 * CHUNKS : 3 * CHUNKS]
    gq, gk, gv, ext = refs[3 * CHUNKS + 3 :]
    pid = pl.program_id(0)
    ext[:, 0:8] = jnp.zeros((3, 8, 128), F32)
    for chunk in range(CHUNKS):
        last, rim, tap = lasts[chunk], rims[chunk], taps[chunk]

        @pl.when(pid == chunk)
        def _():
            def tile(n, _):
                cols = pl.ds(pl.multiple_of(n * 128, 128), 128)
                for at, dst in enumerate((gq, gk, gv)):
                    ext[at, 8:16] = rim[8 * at : 8 * at + 8, cols].astype(F32)
                    total = last[8 * at : 8 * at + 8, cols]
                    for j in range(1, 7):
                        total = total + tap[7 * at + j : 7 * at + j + 1, cols] * ext[at, j : 8 + j]
                    dst[:, cols] = total.astype(BF16)
                return 0

            lax.fori_loop(0, last.shape[1] // 128, tile, 0)


def fold_kernel(me, *refs):
    out = refs[-1]
    share = out.shape[1]
    owners = sum(part.shape[1] for part in refs[:-1]) // 128
    for at in range(refs[0].shape[0] // share):
        for own in range(owners):
            chunk, part = divmod(own, owners // CHUNKS)
            out[owners * at + own] = refs[chunk][
                share * at : share * at + share, 128 * part : 128 * part + 128
            ]


def shift(value, steps):
    count = lax.axis_size(AXES)
    first, last = max(0, -steps), min(count, count - steps)
    return lax.ppermute(value, AXES, [(at, at + steps) for at in range(first, last)])


def gather_own(value):
    return jnp.stack(ring_own(value))


def ring_own(value):
    count = lax.axis_size("own")
    parts = [value]
    for hop in range(1, count):
        parts.append(lax.ppermute(value, "own", [(at, (at + hop) % count) for at in range(count)]))
    return parts


def params_of(vmem):
    return pltpu.CompilerParams(
        dimension_semantics=("arbitrary",), vmem_limit_bytes=vmem
    )


def shards(query, key, value, short_taps, long_taps, decay_rate, residues, grad_out):
    rows, width = query.shape
    owners = lax.axis_size("own")
    per = width // CHUNKS
    steps = per // BLOCK
    quarters = width // owners // BLOCK
    ctx, own = lax.axis_index("ctx"), lax.axis_index("own")
    flat = ctx * owners + own
    half = width // 128
    me = jnp.stack([own, flat // half, flat % half]).astype(jnp.int32)
    table = tables(rows)
    group = BLOCK // 128
    whole = lambda shape: pl.BlockSpec(shape, lambda i, *m: (0,) * len(shape))
    edge = pl.BlockSpec((8, width), lambda i: (rows // 8 - 1, 0))

    rims, short, poles = pl.pallas_call(
        pack_kernel,
        out_shape=(
            jax.ShapeDtypeStruct((24, width), BF16),
            jax.ShapeDtypeStruct((24, 128), F32),
            jax.ShapeDtypeStruct((384, 128), F32),
        ),
        grid=(1,),
        in_specs=[edge] * 3
        + [whole(short_taps.shape), whole(decay_rate.shape), whole(residues.shape), whole(long_taps.shape)],
        out_specs=(
            whole((24, width)),
            whole((24, 128)),
            whole((384, 128)),
        ),
        compiler_params=params_of(60 << 20),
        name="pack",
    )(query, key, value, short_taps, decay_rate, residues, long_taps)
    short_all = gather_own(short)
    rims = shift(rims, 1)
    poles_parts = ring_own(poles)

    def slot(me_ref, chunk):
        return (me_ref[0] - chunk + owners) % owners

    tab = lambda name: (jnp.asarray(table[name]), whole(table[name].shape))
    full = jax.ShapeDtypeStruct((rows, width), BF16)
    part = jax.ShapeDtypeStruct((rows, per), BF16)
    spectrum = jax.ShapeDtypeStruct((2 * rows, per), BF16)
    here = pl.BlockSpec((rows, BLOCK), lambda i, m: (0, i))
    bins = pl.BlockSpec((2 * rows, BLOCK), lambda i, m: (0, i))

    def wide(chunk):
        return pl.BlockSpec((rows, BLOCK), lambda i, m: (0, chunk * steps + i))

    def owned(chunk, i, me_ref):
        return slot(me_ref, chunk * (owners // CHUNKS) + i // quarters)

    def shorts(chunk):
        return pl.BlockSpec((1, 24, 128), lambda i, m: (owned(chunk, i, m), 0, 0))

    def poles_at(chunk, first):
        return pl.BlockSpec(
            (1, 8 * group, 128), lambda i, m: (owned(chunk, i, m), first + i % quarters, 0)
        )

    def call(
        kernel, cost, grid, in_specs, operands, out_shape, out_specs, scratch,
        aliases={}, after=(),
    ):
        known = 1 + len(operands)

        def body(*refs):
            kernel(*refs[:known], *refs[known + len(after) :])

        in_specs = list(in_specs) + [pl.BlockSpec(memory_space=pl.ANY)] * len(after)
        operands = list(operands) + list(after)
        return pl.pallas_call(
            body,
            out_shape=out_shape,
            grid_spec=pltpu.PrefetchScalarGridSpec(
                num_scalar_prefetch=1,
                grid=grid,
                in_specs=in_specs,
                out_specs=out_specs,
                scratch_shapes=scratch,
            ),
            input_output_aliases=aliases,
            compiler_params=params_of(60 << 20),
            cost_estimate=pl.CostEstimate(flops=cost, transcendentals=0, bytes_accessed=cost // 200),
        )(me, *operands)

    spread = jnp.asarray(table["spread"])
    spread_spec = pl.BlockSpec((128, BLOCK), lambda i, m: (0, i % quarters))

    def front(chunk, after):
        moment, moment_spec = tab("moment")
        return call(
            front_kernel, 2_000_000_000, (steps,),
            [wide(chunk)] * 4
            + [pl.BlockSpec((24, BLOCK), lambda i, m: (0, chunk * steps + i)), shorts(chunk), moment_spec, spread_spec],
            (query, key, value, grad_out, rims, short_all, moment, spread),
            (part,) * 5
            + (jax.ShapeDtypeStruct((32, per), F32), jax.ShapeDtypeStruct((24, per), F32)),
            (here,) * 5
            + (
                pl.BlockSpec((32, BLOCK), lambda i, m: (0, i)),
                pl.BlockSpec((24, BLOCK), lambda i, m: (0, i)),
            ),
            [pltpu.VMEM((group, rows + 8, 128), F32)] * 3,
            after=after,
        )

    fronts, behinds, aheads = [], [], []
    for chunk in range(CHUNKS):
        made = front(chunk, [fronts[-1][5]] if fronts else [])
        fronts.append(made)

    def exchange(chunk, after):
        prod, gconv, after = lax.optimization_barrier((fronts[chunk][3], fronts[chunk][4], after))
        behinds.append(shift(prod, 1))
        aheads.append(shift(gconv, -1))
        return after

    poles_all = jnp.stack(exchange(0, tuple(poles_parts)))
    states = call(
        state_kernel, 200_000_000, (1,),
        [whole((32, per))] * CHUNKS + [pl.BlockSpec((owners, 128, 128), lambda i, m: (0, 0, 0))],
        [f[5] for f in fronts] + [poles_all],
        jax.ShapeDtypeStruct((2 * half, 8, 128), BF16),
        whole((2 * half, 8, 128)),
        [],
    )
    arrived = lax.all_to_all(states, AXES, 0, 0, tiled=True)
    for chunk in range(1, CHUNKS):
        exchange(chunk, arrived)

    def mid(chunk, after):
        consts = [tab(name) for name in ("own", "before", "after", "taps", "head", "inverse3")]
        spec32 = pltpu.VMEM((2 * rows, BLOCK), F32)
        spec16 = pltpu.VMEM((2 * rows, BLOCK), BF16)
        return call(
            mid_kernel, 2_000_000_000, (steps,),
            [here] * 4
            + [
                poles_at(chunk, 0),
                poles_at(chunk, quarters),
                pl.BlockSpec((1, 128, 128), lambda i, m: (owned(chunk, i, m), 2, 0)),
            ]
            + [spec for _, spec in consts]
            + [spread_spec],
            [fronts[chunk][3], fronts[chunk][4], behinds[chunk], aheads[chunk]]
            + [poles_all] * 3
            + [c for c, _ in consts]
            + [spread],
            (spectrum,) * 2 + (jax.ShapeDtypeStruct((128, per // CPG), F32),),
            (bins,) * 2 + (pl.BlockSpec((128, 128), lambda i, m: (0, i // quarters)),),
            [spec16]
            + [spec32] * 6
            + [
                spec16,
                pltpu.VMEM((2 * rows, 256), BF16),
                pltpu.VMEM((2 * rows, 128), F32),
                pltpu.VMEM((16, BLOCK), F32),
            ],
            after=after,
        )

    def back(chunk, ys, zs, outs, after):
        consts = [tab(name) for name in ("inverse", "ahead", "behind")]
        made = fronts[chunk]
        operands = [
            made[0], made[1], made[2], grad_out, ys, zs, carried, carried,
            made[6], poles_all, poles_all,
        ] + [c for c, _ in consts]
        in_specs = [
            here, here, here, wide(chunk), bins, bins,
            pl.BlockSpec((group, 8, 128), lambda i, m: (chunk * steps + i, 0, 0)),
            pl.BlockSpec((group, 8, 128), lambda i, m: ((CHUNKS + chunk) * steps + i, 0, 0)),
            pl.BlockSpec((24, BLOCK), lambda i, m: (0, i)),
            poles_at(chunk, 0),
            poles_at(chunk, quarters),
        ] + [spec for _, spec in consts]
        aliases = {}
        for at, out in enumerate(outs):
            aliases[1 + len(operands)] = at
            operands.append(out)
            in_specs.append(pl.BlockSpec(memory_space=pl.ANY))
        ext = pltpu.VMEM((group, rows + 8, 128), F32)
        plain = pltpu.VMEM((rows, BLOCK), F32)
        return call(
            back_kernel, 2_000_000_000, (steps,), in_specs, operands,
            (full,) * 4
            + (jax.ShapeDtypeStruct((24, per), BF16), jax.ShapeDtypeStruct((24, per), F32)),
            (wide(chunk),) * 4
            + (
                pl.BlockSpec((24, BLOCK), lambda i, m: (0, i)),
                pl.BlockSpec((24, BLOCK), lambda i, m: (0, i)),
            ),
            [ext, ext, ext, pltpu.VMEM((32, BLOCK), F32), plain, plain],
            aliases,
            after,
        )

    scanned = call(
        scan_kernel, 200_000_000, (1,),
        [
            whole(arrived.shape),
            pl.BlockSpec(
                (1, 8, 128),
                lambda i, m: (
                    (m[0] - m[2] // (half // owners) + owners) % owners, m[2] % (half // owners), 0
                ),
            ),
        ],
        (arrived, poles_all),
        jax.ShapeDtypeStruct(arrived.shape, BF16),
        whole(arrived.shape),
        [],
    )
    carried = lax.all_to_all(scanned, AXES, 0, 0, tiled=True)

    outs, edges, lasts = (), [], []

    def finish(chunk, after):
        made = back(chunk, mids[chunk][0], mids[chunk][1], outs, after)
        edges.append(shift(made[4], -1))
        lasts.append(made[5])
        return made[:4]

    mids = []
    for chunk in range(CHUNKS):
        mids.append(mid(chunk, [lasts[-1]] if lasts else [scanned]))
        if chunk < CHUNKS - 1:
            outs = finish(chunk, [])
    ctxs = lax.axis_size("ctx")
    share = rows // ctxs
    pieces = call(
        fold_kernel, 100_000_000, (1,),
        [whole((rows, per // CPG))] * CHUNKS,
        [m[2] for m in mids],
        jax.ShapeDtypeStruct((ctxs * owners, share, 128), F32),
        whole((ctxs * owners, share, 128)),
        [],
    )
    landed = lax.all_to_all(pieces, AXES, 0, 0, tiled=True)
    outs = finish(CHUNKS - 1, [landed])
    tokens = rows * ctxs * owners
    total = landed.sum(axis=0) * (1.0 / math.sqrt(tokens * CPG))
    every = lax.all_to_all(
        jnp.broadcast_to(total[None], (ctxs, share, 128)), "ctx", 0, 0, tiled=True
    )

    strip = pl.BlockSpec((8, per), lambda i, m: (rows // 8 - 1, i))
    anyspec = pl.BlockSpec(memory_space=pl.ANY)
    grads = call(
        tail_kernel, 200_000_000, (CHUNKS,),
        [whole((24, per))] * (3 * CHUNKS) + [anyspec] * 3,
        (*lasts, *edges, *[f[6] for f in fronts], *outs[1:4]),
        (full,) * 3,
        (strip,) * 3,
        [pltpu.VMEM((3, 16, 128), F32)],
        {3 * CHUNKS + 1: 0, 3 * CHUNKS + 2: 1, 3 * CHUNKS + 3: 2},
    )
    return (outs[0],) + tuple(grads) + (every.reshape(rows, 128),)


def solution(mesh):
    placed = (
        P(AXES, None),
        P(AXES, None),
        P(AXES, None),
        P(None, None, "own"),
        P(None, "own"),
        P(None, "own"),
        P(None, "own"),
        P(AXES, None),
    )
    return jax.shard_map(
        shards,
        mesh=mesh,
        in_specs=placed,
        out_specs=(P(AXES, None),) * 4 + (P(None, "own"),),
        check_vma=False,
    )
```

```python
import math

import jax
import jax.numpy as jnp
import numpy as np
from jax import lax
from jax.experimental import pallas as pl
from jax.experimental.pallas import tpu as pltpu
from jax.sharding import PartitionSpec as P

CPG = 16
BLOCK = 512
CHUNKS = 2
TERMS = 16
RATE_TOP = 0.03
AXES = ("ctx", "own")
F32, BF16 = jnp.float32, jnp.bfloat16


def split_np(table):
    high = table.astype(np.float32).astype(jnp.bfloat16)
    low = (table - high.astype(np.float64)).astype(np.float32).astype(jnp.bfloat16)
    return high, low


def series(lags):
    nodes = np.cos(np.pi * (np.arange(64) + 0.5) / 64)
    values = np.exp(-np.outer(np.asarray(lags, np.float64), RATE_TOP / 2 * (1 + nodes)))
    basis = np.cos(np.outer(np.arange(TERMS), np.pi * (np.arange(64) + 0.5) / 64))
    coeff = values @ basis.T * (2.0 / 64)
    coeff[:, 0] *= 0.5
    return coeff


def tables(rows):
    angle = np.pi * (2 * np.arange(rows) + 1) / (2 * rows)

    def forward(places):
        phase = np.outer(angle, places)
        return np.concatenate([np.cos(phase), -np.sin(phase)])

    here = np.arange(rows)
    own, before, after = forward(here), forward(here - rows), forward(here + rows)
    phase = np.outer(here, angle)
    inverse = np.concatenate([np.cos(phase), -np.sin(phase)], axis=1) / rows
    cat = np.concatenate
    pair = lambda m: cat(split_np(m), axis=1)

    def triple(m):
        high, low = split_np(m)
        return cat([high, low, high], axis=1)

    return dict(
        own=pair(own),
        before=pair(before),
        after=pair(after),
        taps=triple(own),
        head=triple(own @ series(here)),
        inverse=split_np(inverse)[0],
        inverse3=triple(inverse),
        ahead=triple(series(here + 1)),
        behind=triple(series(rows - here)),
        spread=(np.arange(16 * rows)[None, :] // CPG == here[:, None]).astype(jnp.bfloat16),
        moment=cat(
            [
                pair(series(rows - 1 - here).T),
                pair(series(here).T),
            ],
            axis=0,
        ),
    )


def dot(a, b):
    return jnp.dot(a, b, preferred_element_type=F32)


def halves(x):
    high = x.astype(BF16)
    return high, (x - high.astype(F32)).astype(BF16)


def stack3(x):
    high, low = halves(x)
    return jnp.concatenate([high, high, low], axis=0)


def spread_taps(short, spread):
    high, _ = halves(short)
    rest = short - high.astype(F32)
    mid, low = halves(rest)
    made = dot(jnp.concatenate([high, mid, low], axis=0), spread)
    return made[0:24] + made[24:48] + made[48:72]


def chebyshev(rate):
    z = rate * (2.0 / RATE_TOP) - 1.0
    terms = [jnp.ones_like(z), z]
    while len(terms) < TERMS:
        terms.append(2.0 * z * terms[-1] - terms[-2])
    return terms


def pack_kernel(q, k, v, short, rate, resid, ltaps, small, big, *rims):
    for chunk, rim in enumerate(rims):
        for at, src in enumerate((q, k, v)):
            rim[8 * at : 8 * at + 8] = src[:, rim.shape[1] * chunk : rim.shape[1] * (chunk + 1)]
    small[...] = jnp.zeros_like(small)
    for at in range(3):
        small[7 * at : 7 * at + 7] = short[at]
    for tile in range(rate.shape[1] // 128):
        cols = slice(128 * tile, 128 * tile + 128)
        big[8 * tile : 8 * tile + 8] = rate[:, cols]
        big[128 + 8 * tile : 136 + 8 * tile] = resid[:, cols]
    big[256:] = ltaps[...]


def front_kernel(
    me, q, k, v, g, rim, short, moment, spread,
    qf, kf, vf, prod, gconv, mom, taps, xq, xk, xv,
):
    rows = q.shape[0]
    taps[...] = spread_taps(short[0], spread[...])
    lanes = range(BLOCK // 128)
    for at, (src, dst) in enumerate(((q, xq), (k, xk), (v, xv))):
        for lane in lanes:
            cols = slice(128 * lane, 128 * lane + 128)
            dst[lane, 0:8] = rim[8 * at : 8 * at + 8, cols].astype(F32)
            dst[lane, 8:] = src[:, cols].astype(F32)

    def step(r, _):
        base = pl.multiple_of(r * 32, 32)
        here = pl.ds(base, 32)
        for lane in lanes:
            cols = slice(128 * lane, 128 * lane + 128)
            feats = []
            for at, src in enumerate((xq, xk, xv)):
                total = taps[7 * at : 7 * at + 1, cols] * src[lane, pl.ds(base + 8, 32), :]
                for j in range(1, 7):
                    tap = taps[7 * at + j : 7 * at + j + 1, cols]
                    total = total + tap * src[lane, pl.ds(base + 8 - j, 32), :]
                feats.append(total.astype(BF16))
            qf[here, cols] = feats[0]
            kf[here, cols] = feats[1]
            vf[here, cols] = feats[2]
            prod[here, cols] = (feats[1].astype(F32) * feats[2].astype(F32)).astype(BF16)
            gconv[here, cols] = (g[here, cols].astype(F32) * feats[0].astype(F32)).astype(BF16)
        return 0

    lax.fori_loop(0, rows // 32, step, 0)
    p, c = prod[...], gconv[...]
    mom[0:16] = dot(moment[0:16, :], jnp.concatenate([p, p], axis=0))
    mom[16:32] = dot(moment[16:32, :], jnp.concatenate([c, c], axis=0))


def state_kernel(me, *refs):
    moms, rates, out = refs[:CHUNKS], refs[CHUNKS], refs[CHUNKS + 1]
    owners = rates.shape[0]
    per = out.shape[0] // (2 * owners)
    for own in range(owners):
        chunk, part = divmod(own, owners // CHUNKS)
        mom = moms[chunk]
        slot = (me[0] - own + owners) % owners

        def tile(n, _):
            eight = pl.ds(pl.multiple_of(n * 8, 8), 8)
            cols = pl.ds(pl.multiple_of((part * per + n) * 128, 128), 128)
            terms = chebyshev(rates[slot, eight, :])
            mine = mom[:, cols]
            ahead = terms[0] * mine[0:1]
            back = terms[0] * mine[16:17]
            for at in range(1, TERMS):
                ahead = ahead + terms[at] * mine[at : at + 1]
                back = back + terms[at] * mine[16 + at : 17 + at]
            out[own * per + n] = ahead.astype(BF16)
            out[(owners + own) * per + n] = back.astype(BF16)
            return 0

        lax.fori_loop(0, per, tile, 0, unroll=4)


def scan_kernel(me, states, rates, out):
    count = states.shape[0]
    backward = me[1]
    factor = jnp.exp(rates[0] * -128.0)

    def hop(n, carry):
        at = jnp.where(backward == 1, count - 1 - n, n)
        out[at] = carry.astype(BF16)
        return factor * carry + states[at].astype(F32)

    lax.fori_loop(0, count, hop, jnp.zeros((8, 128), F32), unroll=8)


def modal_weight(rate, resid):
    x = 2.0 * rate
    return resid * jnp.sqrt(x * modal_series(x))


def modal_series(x):
    total = 1.0 - x * (1.0 / 8)
    for n in (7, 6, 5, 4, 3, 2):
        total = 1.0 - x * (1.0 / n) * total
    return total


def mid_kernel(
    me, prod, gconv, before, after, rates, resids, ltaps,
    t_own, t_before, t_after, t_taps, t_head, t_inv3, spread,
    *rest,
):
    (yout, zout, tgrad, xx, own, prv, cur, nxt, tre, hre, cs, tsp, acc, coef) = rest[-14:]
    rows = prod.shape[0]
    quarter = pl.program_id(0) % (128 * CPG // BLOCK)

    @pl.when(quarter == 0)
    def _():
        spec = dot(t_taps[...], stack3(ltaps[0]))
        high, low = halves(spec)
        tsp[:, 0:128] = high
        tsp[:, 128:256] = low
        acc[...] = jnp.zeros_like(acc)

    one_hot = spread[...]
    xx[0:128] = one_hot
    xx[128:256] = one_hot
    tre[...] = dot(tsp[...], xx[...])
    for src, table, dst in (
        (prod, t_own, own), (before, t_before, prv), (gconv, t_own, cur), (after, t_after, nxt),
    ):
        value = src[...]
        xx[0:rows] = value
        xx[rows:] = value
        dst[...] = dot(table[...], xx[...])
    for lane in range(BLOCK // 128):
        cols = slice(128 * lane, 128 * lane + 128)
        eight = slice(8 * lane, 8 * lane + 8)
        weight = modal_weight(rates[0, eight, :], resids[0, eight, :])
        for n, term in enumerate(chebyshev(rates[0, eight, :])):
            coef[n : n + 1, cols] = jnp.sum(term * weight, axis=0, keepdims=True)
    hre[...] = dot(t_head[...], stack3(coef[...]))

    def bins(r, _):
        base = pl.multiple_of(r * 16, 16)
        re = pl.ds(base, 16)
        im = pl.ds(rows + base, 16)
        for lane in range(BLOCK // 128):
            cols = slice(128 * lane, 128 * lane + 128)
            tr, ti, hr, hi = tre[re, cols], tre[im, cols], hre[re, cols], hre[im, cols]
            pr, pi, cr, ci = own[re, cols], own[im, cols], cur[re, cols], cur[im, cols]
            wr, wi = pr + prv[re, cols], pi + prv[im, cols]
            ar, ai = cr + nxt[re, cols], ci + nxt[im, cols]
            yout[re, cols] = (wr * tr - wi * ti + (pr * hr - pi * hi)).astype(BF16)
            yout[im, cols] = (wr * ti + wi * tr + (pr * hi + pi * hr)).astype(BF16)
            zout[re, cols] = (ar * tr + ai * ti + (cr * hr + ci * hi)).astype(BF16)
            zout[im, cols] = (ai * tr - ar * ti + (ci * hr - cr * hi)).astype(BF16)
            cs[re, cols] = (cr * wr + ci * wi).astype(BF16)
            cs[im, cols] = (ci * wr - cr * wi).astype(BF16)
        return 0

    lax.fori_loop(0, rows // 16, bins, 0)
    acc[...] += lax.dot_general(
        cs[...], spread[...], (((1,), (1,)), ((), ())), preferred_element_type=F32
    )

    @pl.when(quarter == 128 * CPG // BLOCK - 1)
    def _():
        made = dot(t_inv3[...], stack3(acc[...]))
        share = tgrad.shape[2]
        for at in range(tgrad.shape[0]):
            tgrad[at, 0] = made[share * at : share * at + share]


def back_kernel(
    me, qf, kf, vf, g, ys, zs, sf, sb, taps, rates, resids,
    t_inv, t_ahead, t_behind, *rest,
):
    (layer, gq, gk, gv, rim, last, eq, ek, ev, coef, lg, gp) = rest[-12:]
    rows = qf.shape[0]
    lanes = range(BLOCK // 128)
    for lane in lanes:
        cols = slice(128 * lane, 128 * lane + 128)
        eight = slice(8 * lane, 8 * lane + 8)
        weight = modal_weight(rates[0, eight, :], resids[0, eight, :])
        sets = (weight * sf[lane].astype(F32), weight * sb[lane].astype(F32))
        for n, term in enumerate(chebyshev(rates[0, eight, :])):
            for at, field in enumerate(sets):
                coef[16 * at + n : 16 * at + n + 1, cols] = jnp.sum(
                    term * field, axis=0, keepdims=True
                )
    lg[...] = dot(t_inv[...], ys[...]) + dot(t_ahead[...], stack3(coef[0:16]))
    gp[...] = dot(t_inv[...], zs[...]) + dot(t_behind[...], stack3(coef[16:32]))

    def rows_out(r, _):
        here = pl.ds(pl.multiple_of(r * 16, 16), 16)
        for lane in lanes:
            cols = slice(128 * lane, 128 * lane + 128)
            conv, grad = lg[here, cols], gp[here, cols]
            layer[here, cols] = (qf[here, cols].astype(F32) * conv).astype(BF16)
            eq[lane, here] = (g[here, cols].astype(F32) * conv).astype(BF16).astype(F32)
            ek[lane, here] = (grad * vf[here, cols].astype(F32)).astype(BF16).astype(F32)
            ev[lane, here] = (grad * kf[here, cols].astype(F32)).astype(BF16).astype(F32)
        return 0

    lax.fori_loop(0, rows // 16, rows_out, 0)
    for at, src in enumerate((eq, ek, ev)):
        for lane in lanes:
            cols = slice(128 * lane, 128 * lane + 128)
            src[lane, rows:] = jnp.zeros((8, 128), F32)
            rim[8 * at : 8 * at + 8, cols] = src[lane, 0:8].astype(BF16)

    def finish(r, _):
        base = pl.multiple_of(r * 32, 32)
        here = pl.ds(base, 32)
        for lane in lanes:
            cols = slice(128 * lane, 128 * lane + 128)
            for at, (src, dst) in enumerate(((eq, gq), (ek, gk), (ev, gv))):
                total = taps[7 * at : 7 * at + 1, cols] * src[lane, here, :]
                for j in range(1, 7):
                    tap = taps[7 * at + j : 7 * at + j + 1, cols]
                    total = total + tap * src[lane, pl.ds(base + j, 32), :]
                dst[here, cols] = total.astype(BF16)
                last[8 * at : 8 * at + 8, cols] = total[24:32]
        return 0

    lax.fori_loop(0, rows // 32, finish, 0)


def tail_kernel(me, *refs):
    lasts, rims, taps = refs[:CHUNKS], refs[CHUNKS : 2 * CHUNKS], refs[2 * CHUNKS : 3 * CHUNKS]
    gq, gk, gv, ext = refs[3 * CHUNKS + 3 :]
    piece = pl.program_id(0) // (pl.num_programs(0) // CHUNKS)
    ext[:, 0:8] = jnp.zeros((3, 8, 128), F32)
    for chunk in range(CHUNKS):
        last, rim, tap = lasts[chunk], rims[chunk], taps[chunk]

        @pl.when(piece == chunk)
        def _():
            def tile(n, _):
                cols = pl.ds(pl.multiple_of(n * 128, 128), 128)
                for at, dst in enumerate((gq, gk, gv)):
                    ext[at, 8:16] = rim[8 * at : 8 * at + 8, cols].astype(F32)
                    total = last[8 * at : 8 * at + 8, cols]
                    for j in range(1, 7):
                        total = total + tap[7 * at + j : 7 * at + j + 1, cols] * ext[at, j : 8 + j]
                    dst[:, cols] = total.astype(BF16)
                return 0

            lax.fori_loop(0, last.shape[1] // 128, tile, 0)


def shift(value, steps):
    count = lax.axis_size(AXES)
    first, last = max(0, -steps), min(count, count - steps)
    return lax.ppermute(value, AXES, [(at, at + steps) for at in range(first, last)])


def gather_own(value):
    return jnp.stack(ring_own(value))


def ring_own(value):
    count = lax.axis_size("own")
    parts = [value]
    for hop in range(1, count):
        parts.append(lax.ppermute(value, "own", [(at, (at + hop) % count) for at in range(count)]))
    return parts


def params_of(vmem):
    return pltpu.CompilerParams(
        dimension_semantics=("arbitrary",), vmem_limit_bytes=vmem
    )


def shards(query, key, value, short_taps, long_taps, decay_rate, residues, grad_out):
    rows, width = query.shape
    owners = lax.axis_size("own")
    per = width // CHUNKS
    steps = per // BLOCK
    quarters = width // owners // BLOCK
    ctx, own = lax.axis_index("ctx"), lax.axis_index("own")
    flat = ctx * owners + own
    half = width // 128
    me = jnp.stack([own, flat // half, flat % half]).astype(jnp.int32)
    table = tables(rows)
    group = BLOCK // 128
    whole = lambda shape: pl.BlockSpec(shape, lambda i, *m: (0,) * len(shape))
    edge = pl.BlockSpec((8, width), lambda i: (rows // 8 - 1, 0))

    short, poles, *rims = pl.pallas_call(
        pack_kernel,
        out_shape=(
            jax.ShapeDtypeStruct((24, 128), F32),
            jax.ShapeDtypeStruct((384, 128), F32),
        )
        + (jax.ShapeDtypeStruct((24, per), BF16),) * CHUNKS,
        grid=(1,),
        in_specs=[edge] * 3
        + [whole(short_taps.shape), whole(decay_rate.shape), whole(residues.shape), whole(long_taps.shape)],
        out_specs=(
            whole((24, 128)),
            whole((384, 128)),
        )
        + (whole((24, per)),) * CHUNKS,
        compiler_params=params_of(60 << 20),
        name="pack",
    )(query, key, value, short_taps, decay_rate, residues, long_taps)
    rims[0] = shift(rims[0], 1)
    short_all = gather_own(short)
    poles_parts = ring_own(poles)
    for chunk in range(1, CHUNKS):
        edge_rows, _ = lax.optimization_barrier((rims[chunk], short_all))
        rims[chunk] = shift(edge_rows, 1)

    def slot(me_ref, chunk):
        return (me_ref[0] - chunk + owners) % owners

    tab = lambda name: (jnp.asarray(table[name]), whole(table[name].shape))
    full = jax.ShapeDtypeStruct((rows, width), BF16)
    part = jax.ShapeDtypeStruct((rows, per), BF16)
    spectrum = jax.ShapeDtypeStruct((2 * rows, per), BF16)
    here = pl.BlockSpec((rows, BLOCK), lambda i, m: (0, i))
    bins = pl.BlockSpec((2 * rows, BLOCK), lambda i, m: (0, i))

    def wide(chunk):
        return pl.BlockSpec((rows, BLOCK), lambda i, m: (0, chunk * steps + i))

    def owned(chunk, i, me_ref):
        return slot(me_ref, chunk * (owners // CHUNKS) + i // quarters)

    def shorts(chunk):
        return pl.BlockSpec((1, 24, 128), lambda i, m: (owned(chunk, i, m), 0, 0))

    def poles_at(chunk, first):
        return pl.BlockSpec(
            (1, 8 * group, 128), lambda i, m: (owned(chunk, i, m), first + i % quarters, 0)
        )

    def call(
        kernel, cost, grid, in_specs, operands, out_shape, out_specs, scratch,
        aliases={}, after=(),
    ):
        known = 1 + len(operands)

        def body(*refs):
            kernel(*refs[:known], *refs[known + len(after) :])

        in_specs = list(in_specs) + [pl.BlockSpec(memory_space=pl.ANY)] * len(after)
        operands = list(operands) + list(after)
        return pl.pallas_call(
            body,
            out_shape=out_shape,
            grid_spec=pltpu.PrefetchScalarGridSpec(
                num_scalar_prefetch=1,
                grid=grid,
                in_specs=in_specs,
                out_specs=out_specs,
                scratch_shapes=scratch,
            ),
            input_output_aliases=aliases,
            compiler_params=params_of(60 << 20),
            cost_estimate=pl.CostEstimate(flops=cost, transcendentals=0, bytes_accessed=cost // 200),
        )(me, *operands)

    spread = jnp.asarray(table["spread"])
    spread_spec = pl.BlockSpec((128, BLOCK), lambda i, m: (0, i % quarters))

    def front(chunk, after):
        moment, moment_spec = tab("moment")
        return call(
            front_kernel, 2_000_000_000, (steps,),
            [wide(chunk)] * 4
            + [pl.BlockSpec((24, BLOCK), lambda i, m: (0, i)), shorts(chunk), moment_spec, spread_spec],
            (query, key, value, grad_out, rims[chunk], short_all, moment, spread),
            (part,) * 5
            + (jax.ShapeDtypeStruct((32, per), F32), jax.ShapeDtypeStruct((24, per), F32)),
            (here,) * 5
            + (
                pl.BlockSpec((32, BLOCK), lambda i, m: (0, i)),
                pl.BlockSpec((24, BLOCK), lambda i, m: (0, i)),
            ),
            [pltpu.VMEM((group, rows + 8, 128), F32)] * 3,
            after=after,
        )

    fronts, behinds, aheads = [], [], []
    for chunk in range(CHUNKS):
        made = front(chunk, [fronts[-1][5]] if fronts else [])
        fronts.append(made)

    def exchange(chunk, after):
        prod, gconv, after = lax.optimization_barrier((fronts[chunk][3], fronts[chunk][4], after))
        behinds.append(shift(prod, 1))
        aheads.append(shift(gconv, -1))
        return after

    poles_all = jnp.stack(exchange(0, tuple(poles_parts)))
    states = call(
        state_kernel, 200_000_000, (1,),
        [whole((32, per))] * CHUNKS + [pl.BlockSpec((owners, 128, 128), lambda i, m: (0, 0, 0))],
        [f[5] for f in fronts] + [poles_all],
        jax.ShapeDtypeStruct((2 * half, 8, 128), BF16),
        whole((2 * half, 8, 128)),
        [],
    )
    arrived = lax.all_to_all(states, AXES, 0, 0, tiled=True)
    for chunk in range(1, CHUNKS):
        exchange(chunk, states)
    ctxs = lax.axis_size("ctx")
    share = rows // ctxs

    def mid(chunk, pieces, after):
        consts = [tab(name) for name in ("own", "before", "after", "taps", "head", "inverse3")]
        spec32 = pltpu.VMEM((2 * rows, BLOCK), F32)
        spec16 = pltpu.VMEM((2 * rows, BLOCK), BF16)
        return call(
            mid_kernel, 2_000_000_000, (steps,),
            [here] * 4
            + [
                poles_at(chunk, 0),
                poles_at(chunk, quarters),
                pl.BlockSpec((1, 128, 128), lambda i, m: (owned(chunk, i, m), 2, 0)),
            ]
            + [spec for _, spec in consts]
            + [spread_spec]
            + [pl.BlockSpec(memory_space=pl.ANY)] * len(pieces),
            [fronts[chunk][3], fronts[chunk][4], behinds[chunk], aheads[chunk]]
            + [poles_all] * 3
            + [c for c, _ in consts]
            + [spread]
            + pieces,
            (spectrum,) * 2 + (jax.ShapeDtypeStruct((ctxs, owners, share, 128), F32),),
            (bins,) * 2
            + (
                pl.BlockSpec(
                    (ctxs, 1, share, 128),
                    lambda i, m: (0, chunk * (owners // CHUNKS) + i // quarters, 0, 0),
                ),
            ),
            [spec16]
            + [spec32] * 6
            + [
                spec16,
                pltpu.VMEM((2 * rows, 256), BF16),
                pltpu.VMEM((2 * rows, 128), F32),
                pltpu.VMEM((16, BLOCK), F32),
            ],
            {8 + len(consts) + 1: 2} if pieces else {},
            after,
        )

    def back(chunk, ys, zs, outs, after):
        consts = [tab(name) for name in ("inverse", "ahead", "behind")]
        made = fronts[chunk]
        operands = [
            made[0], made[1], made[2], grad_out, ys, zs, carried, carried,
            made[6], poles_all, poles_all,
        ] + [c for c, _ in consts]
        in_specs = [
            here, here, here, wide(chunk), bins, bins,
            pl.BlockSpec((group, 8, 128), lambda i, m: (chunk * steps + i, 0, 0)),
            pl.BlockSpec((group, 8, 128), lambda i, m: ((CHUNKS + chunk) * steps + i, 0, 0)),
            pl.BlockSpec((24, BLOCK), lambda i, m: (0, i)),
            poles_at(chunk, 0),
            poles_at(chunk, quarters),
        ] + [spec for _, spec in consts]
        aliases = {}
        for at, out in enumerate(outs):
            aliases[1 + len(operands)] = at
            operands.append(out)
            in_specs.append(pl.BlockSpec(memory_space=pl.ANY))
        ext = pltpu.VMEM((group, rows + 8, 128), F32)
        plain = pltpu.VMEM((rows, BLOCK), F32)
        return call(
            back_kernel, 2_000_000_000, (steps,), in_specs, operands,
            (full,) * 4
            + (jax.ShapeDtypeStruct((24, per), BF16), jax.ShapeDtypeStruct((24, per), F32)),
            (wide(chunk),) * 4
            + (
                pl.BlockSpec((24, BLOCK), lambda i, m: (0, i)),
                pl.BlockSpec((24, BLOCK), lambda i, m: (0, i)),
            ),
            [ext, ext, ext, pltpu.VMEM((32, BLOCK), F32), plain, plain],
            aliases,
            after,
        )

    mids = [mid(0, [], [])]
    scanned = call(
        scan_kernel, 200_000_000, (1,),
        [
            whole(arrived.shape),
            pl.BlockSpec(
                (1, 8, 128),
                lambda i, m: (
                    (m[0] - m[2] // (half // owners) + owners) % owners, m[2] % (half // owners), 0
                ),
            ),
        ],
        (arrived, poles_all),
        jax.ShapeDtypeStruct(arrived.shape, BF16),
        whole(arrived.shape),
        [],
        after=[mids[0][2]],
    )
    carried = lax.all_to_all(scanned, AXES, 0, 0, tiled=True)

    outs, edges, lasts = (), [], []

    def finish(chunk, after):
        made = back(chunk, mids[chunk][0], mids[chunk][1], outs, after)
        edges.append(shift(made[4], -1))
        lasts.append(made[5])
        return made[:4]

    for chunk in range(1, CHUNKS):
        mids.append(mid(chunk, [mids[-1][2]], [scanned]))
    landed = lax.all_to_all(mids[-1][2].reshape(ctxs * owners, share, 128), AXES, 0, 0, tiled=True)
    for chunk in range(CHUNKS):
        outs = finish(chunk, [])
    tokens = rows * ctxs * owners
    total = landed.sum(axis=0) * (1.0 / math.sqrt(tokens * CPG))
    every = lax.all_to_all(
        jnp.broadcast_to(total[None], (ctxs, share, 128)), "ctx", 0, 0, tiled=True
    )

    cuts = 2
    strip = pl.BlockSpec((8, per // cuts), lambda i, m: (rows // 8 - 1, i))
    bands = [
        pl.BlockSpec(
            (24, per // cuts),
            lambda i, m, chunk=chunk: (0, jnp.clip(i - cuts * chunk, 0, cuts - 1)),
        )
        for chunk in range(CHUNKS)
    ]
    anyspec = pl.BlockSpec(memory_space=pl.ANY)
    grads = call(
        tail_kernel, 200_000_000, (CHUNKS * cuts,),
        bands * 3 + [anyspec] * 3,
        (*lasts, *edges, *[f[6] for f in fronts], *outs[1:4]),
        (full,) * 3,
        (strip,) * 3,
        [pltpu.VMEM((3, 16, 128), F32)],
        {3 * CHUNKS + 1: 0, 3 * CHUNKS + 2: 1, 3 * CHUNKS + 3: 2},
    )
    return (outs[0],) + tuple(grads) + (every.reshape(rows, 128),)


def solution(mesh):
    placed = (
        P(AXES, None),
        P(AXES, None),
        P(AXES, None),
        P(None, None, "own"),
        P(None, "own"),
        P(None, "own"),
        P(None, "own"),
        P(AXES, None),
    )
    return jax.shard_map(
        shards,
        mesh=mesh,
        in_specs=placed,
        out_specs=(P(AXES, None),) * 4 + (P(None, "own"),),
        check_vma=False,
    )
```

```python
import functools
import math

import jax
import jax.numpy as jnp
import numpy as np
from jax import lax
from jax.experimental import pallas as pl
from jax.experimental.pallas import tpu as pltpu
from jax.sharding import PartitionSpec as P

CPG = 16
BLOCK = 512
CHUNKS = 2
TERMS = 16
RATE_TOP = 0.03
AXES = ("ctx", "own")
F32, BF16 = jnp.float32, jnp.bfloat16


def split_np(table):
    high = table.astype(np.float32).astype(jnp.bfloat16)
    low = (table - high.astype(np.float64)).astype(np.float32).astype(jnp.bfloat16)
    return high, low


def series(lags):
    nodes = np.cos(np.pi * (np.arange(64) + 0.5) / 64)
    values = np.exp(-np.outer(np.asarray(lags, np.float64), RATE_TOP / 2 * (1 + nodes)))
    basis = np.cos(np.outer(np.arange(TERMS), np.pi * (np.arange(64) + 0.5) / 64))
    coeff = values @ basis.T * (2.0 / 64)
    coeff[:, 0] *= 0.5
    return coeff


def tables(rows):
    angle = np.pi * (2 * np.arange(rows) + 1) / (2 * rows)

    def forward(places):
        phase = np.outer(angle, places)
        return np.concatenate([np.cos(phase), -np.sin(phase)])

    here = np.arange(rows)
    own, before, after = forward(here), forward(here - rows), forward(here + rows)
    phase = np.outer(here, angle)
    inverse = np.concatenate([np.cos(phase), -np.sin(phase)], axis=1) / rows
    cat = np.concatenate
    pair = lambda m: cat(split_np(m), axis=1)

    def triple(m):
        high, low = split_np(m)
        return cat([high, low, high], axis=1)

    return dict(
        own=pair(own),
        before=pair(before),
        after=pair(after),
        taps=triple(own),
        head=triple(own @ series(here)),
        inverse=split_np(inverse)[0],
        inverse3=triple(inverse),
        ahead=triple(series(here + 1)),
        behind=triple(series(rows - here)),
        spread=(np.arange(16 * rows)[None, :] // CPG == here[:, None]).astype(jnp.bfloat16),
        moment=cat(
            [
                pair(series(rows - 1 - here).T),
                pair(series(here).T),
            ],
            axis=0,
        ),
    )


def dot(a, b):
    return jnp.dot(a, b, preferred_element_type=F32)


def halves(x):
    high = x.astype(BF16)
    return high, (x - high.astype(F32)).astype(BF16)


def stack3(x):
    high, low = halves(x)
    return jnp.concatenate([high, high, low], axis=0)


def spread_taps(short, spread):
    high, _ = halves(short)
    rest = short - high.astype(F32)
    mid, low = halves(rest)
    made = dot(jnp.concatenate([high, mid, low], axis=0), spread)
    return made[0:24] + made[24:48] + made[48:72]


def chebyshev(rate):
    z = rate * (2.0 / RATE_TOP) - 1.0
    terms = [jnp.ones_like(z), z]
    while len(terms) < TERMS:
        terms.append(2.0 * z * terms[-1] - terms[-2])
    return terms


def pack_kernel(q, k, v, short, rate, resid, ltaps, small, big, *rims):
    for chunk, rim in enumerate(rims):
        for at, src in enumerate((q, k, v)):
            rim[8 * at : 8 * at + 8] = src[:, rim.shape[1] * chunk : rim.shape[1] * (chunk + 1)]
    small[...] = jnp.zeros_like(small)
    for at in range(3):
        small[7 * at : 7 * at + 7] = short[at]
    for tile in range(rate.shape[1] // 128):
        cols = slice(128 * tile, 128 * tile + 128)
        big[8 * tile : 8 * tile + 8] = rate[:, cols]
        big[128 + 8 * tile : 136 + 8 * tile] = resid[:, cols]
    big[256:] = ltaps[...]


def front_kernel(
    me, q, k, v, g, rim, short, moment, spread, *rest, pieces=0
):
    moms, rates = rest[: max(pieces - 1, 0)], rest[max(pieces - 1, 0) : max(2 * pieces - 1, 0)]
    outs = rest[len(moms) + len(rates) :]
    qf, kf, vf, prod, gconv, mom, taps = outs[:7]
    xq, xk, xv = outs[-3:]
    rows = q.shape[0]
    taps[...] = spread_taps(short[0], spread[...])
    lanes = range(BLOCK // 128)
    for at, (src, dst) in enumerate(((q, xq), (k, xk), (v, xv))):
        for lane in lanes:
            cols = slice(128 * lane, 128 * lane + 128)
            dst[lane, 0:8] = rim[8 * at : 8 * at + 8, cols].astype(F32)
            dst[lane, 8:] = src[:, cols].astype(F32)

    def step(r, _):
        base = pl.multiple_of(r * 32, 32)
        here = pl.ds(base, 32)
        for lane in lanes:
            cols = slice(128 * lane, 128 * lane + 128)
            feats = []
            for at, src in enumerate((xq, xk, xv)):
                total = taps[7 * at : 7 * at + 1, cols] * src[lane, pl.ds(base + 8, 32), :]
                for j in range(1, 7):
                    tap = taps[7 * at + j : 7 * at + j + 1, cols]
                    total = total + tap * src[lane, pl.ds(base + 8 - j, 32), :]
                feats.append(total.astype(BF16))
            qf[here, cols] = feats[0]
            kf[here, cols] = feats[1]
            vf[here, cols] = feats[2]
            prod[here, cols] = (feats[1].astype(F32) * feats[2].astype(F32)).astype(BF16)
            gconv[here, cols] = (g[here, cols].astype(F32) * feats[0].astype(F32)).astype(BF16)
        return 0

    lax.fori_loop(0, rows // 32, step, 0)
    p, c = prod[...], gconv[...]
    mom[0:16] = dot(moment[0:16, :], jnp.concatenate([p, p], axis=0))
    mom[16:32] = dot(moment[16:32, :], jnp.concatenate([c, c], axis=0))
    for piece in range(pieces):
        source, states = (*moms, mom)[piece], outs[7]
        for lane in lanes:
            mine = source[:, 128 * lane : 128 * lane + 128]
            terms = chebyshev(rates[piece][0, 8 * lane : 8 * lane + 8, :])
            ahead = terms[0] * mine[0:1]
            back = terms[0] * mine[16:17]
            for at in range(1, TERMS):
                ahead = ahead + terms[at] * mine[at : at + 1]
                back = back + terms[at] * mine[16 + at : 17 + at]
            states[0, piece, lane] = ahead.astype(BF16)
            states[1, piece, lane] = back.astype(BF16)


def scan_kernel(me, states, rates, out):
    count = states.shape[0]
    backward = me[1]
    factor = jnp.exp(rates[0] * -128.0)

    def hop(n, carry):
        at = jnp.where(backward == 1, count - 1 - n, n)
        out[at] = carry.astype(BF16)
        return factor * carry + states[at].astype(F32)

    lax.fori_loop(0, count, hop, jnp.zeros((8, 128), F32), unroll=8)


def modal_weight(rate, resid):
    x = 2.0 * rate
    return resid * jnp.sqrt(x * modal_series(x))


def modal_series(x):
    total = 1.0 - x * (1.0 / 8)
    for n in (7, 6, 5, 4, 3, 2):
        total = 1.0 - x * (1.0 / n) * total
    return total


def mid_kernel(
    me, prod, gconv, before, after, rates, resids, ltaps,
    t_own, t_before, t_after, t_taps, t_head, t_inv3, spread,
    *rest,
):
    (yout, zout, tgrad, xx, own, prv, cur, nxt, tre, hre, cs, tsp, acc, coef) = rest[-14:]
    rows = prod.shape[0]
    quarter = pl.program_id(0) % (128 * CPG // BLOCK)

    @pl.when(quarter == 0)
    def _():
        spec = dot(t_taps[...], stack3(ltaps[0]))
        high, low = halves(spec)
        tsp[:, 0:128] = high
        tsp[:, 128:256] = low
        acc[...] = jnp.zeros_like(acc)

    one_hot = spread[...]
    xx[0:128] = one_hot
    xx[128:256] = one_hot
    for lane in range(BLOCK // 128):
        cols = slice(128 * lane, 128 * lane + 128)
        eight = slice(8 * lane, 8 * lane + 8)
        weight = modal_weight(rates[0, eight, :], resids[0, eight, :])
        for n, term in enumerate(chebyshev(rates[0, eight, :])):
            coef[n : n + 1, cols] = jnp.sum(term * weight, axis=0, keepdims=True)

    def transforms(half):
        wide = slice(256 * half, 256 * half + 256)
        tre[:, wide] = dot(tsp[...], xx[:, wide])
        for src, table, dst in (
            (prod, t_own, own), (before, t_before, prv), (gconv, t_own, cur), (after, t_after, nxt),
        ):
            value = src[:, wide]
            dst[:, wide] = dot(table[...], jnp.concatenate([value, value], axis=0))
        hre[:, wide] = dot(t_head[...], stack3(coef[:, wide]))

    def bins(base, lane):
        re = slice(base, base + 16)
        im = slice(rows + base, rows + base + 16)
        cols = slice(128 * lane, 128 * lane + 128)
        tr, ti, hr, hi = tre[re, cols], tre[im, cols], hre[re, cols], hre[im, cols]
        pr, pi, cr, ci = own[re, cols], own[im, cols], cur[re, cols], cur[im, cols]
        wr, wi = pr + prv[re, cols], pi + prv[im, cols]
        ar, ai = cr + nxt[re, cols], ci + nxt[im, cols]
        yout[re, cols] = (wr * tr - wi * ti + (pr * hr - pi * hi)).astype(BF16)
        yout[im, cols] = (wr * ti + wi * tr + (pr * hi + pi * hr)).astype(BF16)
        zout[re, cols] = (ar * tr + ai * ti + (cr * hr + ci * hi)).astype(BF16)
        zout[im, cols] = (ai * tr - ar * ti + (ci * hr - cr * hi)).astype(BF16)
        cs[re, cols] = (cr * wr + ci * wi).astype(BF16)
        cs[im, cols] = (ci * wr - cr * wi).astype(BF16)

    for half in range(BLOCK // 256):
        transforms(half)
        for lane in (2 * half, 2 * half + 1):
            for base in range(0, rows, 16):
                bins(base, lane)
    acc[...] += lax.dot_general(
        cs[...], spread[...], (((1,), (1,)), ((), ())), preferred_element_type=F32
    )

    @pl.when(quarter == 128 * CPG // BLOCK - 1)
    def _():
        made = dot(t_inv3[...], stack3(acc[...]))
        share = tgrad.shape[2]
        for at in range(tgrad.shape[0]):
            tgrad[at, 0] = made[share * at : share * at + share]


def back_kernel(
    me, qf, kf, vf, g, ys, zs, sf, sb, taps, rates, resids,
    t_inv, t_ahead, t_behind, *rest,
):
    (layer, gq, gk, gv, rim, last, eq, ek, ev, coef, lg, gp) = rest[-12:]
    rows = qf.shape[0]
    lanes = range(BLOCK // 128)
    for lane in lanes:
        cols = slice(128 * lane, 128 * lane + 128)
        eight = slice(8 * lane, 8 * lane + 8)
        weight = modal_weight(rates[0, eight, :], resids[0, eight, :])
        sets = (weight * sf[lane].astype(F32), weight * sb[lane].astype(F32))
        for n, term in enumerate(chebyshev(rates[0, eight, :])):
            for at, field in enumerate(sets):
                coef[16 * at + n : 16 * at + n + 1, cols] = jnp.sum(
                    term * field, axis=0, keepdims=True
                )
    lg[...] = dot(t_inv[...], ys[...]) + dot(t_ahead[...], stack3(coef[0:16]))
    gp[...] = dot(t_inv[...], zs[...]) + dot(t_behind[...], stack3(coef[16:32]))

    def rows_out(r, _):
        here = pl.ds(pl.multiple_of(r * 16, 16), 16)
        for lane in lanes:
            cols = slice(128 * lane, 128 * lane + 128)
            conv, grad = lg[here, cols], gp[here, cols]
            layer[here, cols] = (qf[here, cols].astype(F32) * conv).astype(BF16)
            eq[lane, here] = (g[here, cols].astype(F32) * conv).astype(BF16).astype(F32)
            ek[lane, here] = (grad * vf[here, cols].astype(F32)).astype(BF16).astype(F32)
            ev[lane, here] = (grad * kf[here, cols].astype(F32)).astype(BF16).astype(F32)
        return 0

    lax.fori_loop(0, rows // 16, rows_out, 0)
    for at, src in enumerate((eq, ek, ev)):
        for lane in lanes:
            cols = slice(128 * lane, 128 * lane + 128)
            src[lane, rows:] = jnp.zeros((8, 128), F32)
            rim[8 * at : 8 * at + 8, cols] = src[lane, 0:8].astype(BF16)

    def finish(r, _):
        base = pl.multiple_of(r * 32, 32)
        here = pl.ds(base, 32)
        for lane in lanes:
            cols = slice(128 * lane, 128 * lane + 128)
            for at, (src, dst) in enumerate(((eq, gq), (ek, gk), (ev, gv))):
                total = taps[7 * at : 7 * at + 1, cols] * src[lane, here, :]
                for j in range(1, 7):
                    tap = taps[7 * at + j : 7 * at + j + 1, cols]
                    total = total + tap * src[lane, pl.ds(base + j, 32), :]
                dst[here, cols] = total.astype(BF16)
                last[8 * at : 8 * at + 8, cols] = total[24:32]
        return 0

    lax.fori_loop(0, rows // 32, finish, 0)


def tail_kernel(me, *refs):
    lasts, rims, taps = refs[:CHUNKS], refs[CHUNKS : 2 * CHUNKS], refs[2 * CHUNKS : 3 * CHUNKS]
    gq, gk, gv, ext = refs[3 * CHUNKS + 3 :]
    piece = pl.program_id(0) // (pl.num_programs(0) // CHUNKS)
    ext[:, 0:8] = jnp.zeros((3, 8, 128), F32)
    for chunk in range(CHUNKS):
        last, rim, tap = lasts[chunk], rims[chunk], taps[chunk]

        @pl.when(piece == chunk)
        def _():
            def tile(n, _):
                cols = pl.ds(pl.multiple_of(n * 128, 128), 128)
                for at, dst in enumerate((gq, gk, gv)):
                    ext[at, 8:16] = rim[8 * at : 8 * at + 8, cols].astype(F32)
                    total = last[8 * at : 8 * at + 8, cols]
                    for j in range(1, 7):
                        total = total + tap[7 * at + j : 7 * at + j + 1, cols] * ext[at, j : 8 + j]
                    dst[:, cols] = total.astype(BF16)
                return 0

            lax.fori_loop(0, last.shape[1] // 128, tile, 0, unroll=4)


def shift(value, steps):
    count = lax.axis_size(AXES)
    first, last = max(0, -steps), min(count, count - steps)
    return lax.ppermute(value, AXES, [(at, at + steps) for at in range(first, last)])


def gather_own(value):
    return jnp.stack(ring_own(value))


def ring_own(value):
    count = lax.axis_size("own")
    parts = [value]
    for hop in range(1, count):
        parts.append(lax.ppermute(value, "own", [(at, (at + hop) % count) for at in range(count)]))
    return parts


def params_of(vmem):
    return pltpu.CompilerParams(
        dimension_semantics=("arbitrary",), vmem_limit_bytes=vmem
    )


def shards(query, key, value, short_taps, long_taps, decay_rate, residues, grad_out):
    rows, width = query.shape
    owners = lax.axis_size("own")
    per = width // CHUNKS
    steps = per // BLOCK
    quarters = width // owners // BLOCK
    ctx, own = lax.axis_index("ctx"), lax.axis_index("own")
    flat = ctx * owners + own
    half = width // 128
    me = jnp.stack([own, flat // half, flat % half]).astype(jnp.int32)
    table = tables(rows)
    group = BLOCK // 128
    whole = lambda shape: pl.BlockSpec(shape, lambda i, *m: (0,) * len(shape))
    edge = pl.BlockSpec((8, width), lambda i: (rows // 8 - 1, 0))

    short, poles, *rims = pl.pallas_call(
        pack_kernel,
        out_shape=(
            jax.ShapeDtypeStruct((24, 128), F32),
            jax.ShapeDtypeStruct((384, 128), F32),
        )
        + (jax.ShapeDtypeStruct((24, per), BF16),) * CHUNKS,
        grid=(1,),
        in_specs=[edge] * 3
        + [whole(short_taps.shape), whole(decay_rate.shape), whole(residues.shape), whole(long_taps.shape)],
        out_specs=(
            whole((24, 128)),
            whole((384, 128)),
        )
        + (whole((24, per)),) * CHUNKS,
        compiler_params=params_of(60 << 20),
        name="pack",
    )(query, key, value, short_taps, decay_rate, residues, long_taps)
    rims[0] = shift(rims[0], 1)
    short_all = gather_own(short)
    poles_parts = ring_own(poles)
    for chunk in range(1, CHUNKS):
        edge_rows, _ = lax.optimization_barrier((rims[chunk], short_all))
        rims[chunk] = shift(edge_rows, 1)

    def slot(me_ref, chunk):
        return (me_ref[0] - chunk + owners) % owners

    tab = lambda name: (jnp.asarray(table[name]), whole(table[name].shape))
    full = jax.ShapeDtypeStruct((rows, width), BF16)
    part = jax.ShapeDtypeStruct((rows, per), BF16)
    spectrum = jax.ShapeDtypeStruct((2 * rows, per), BF16)
    here = pl.BlockSpec((rows, BLOCK), lambda i, m: (0, i))
    bins = pl.BlockSpec((2 * rows, BLOCK), lambda i, m: (0, i))

    def wide(chunk):
        return pl.BlockSpec((rows, BLOCK), lambda i, m: (0, chunk * steps + i))

    def owned(chunk, i, me_ref):
        return slot(me_ref, chunk * (owners // CHUNKS) + i // quarters)

    def shorts(chunk):
        return pl.BlockSpec((1, 24, 128), lambda i, m: (owned(chunk, i, m), 0, 0))

    def poles_at(chunk, first):
        return pl.BlockSpec(
            (1, 8 * group, 128), lambda i, m: (owned(chunk, i, m), first + i % quarters, 0)
        )

    def call(
        kernel, cost, grid, in_specs, operands, out_shape, out_specs, scratch,
        aliases={}, after=(),
    ):
        known = 1 + len(operands)

        def body(*refs):
            kernel(*refs[:known], *refs[known + len(after) :])

        in_specs = list(in_specs) + [pl.BlockSpec(memory_space=pl.ANY)] * len(after)
        operands = list(operands) + list(after)
        return pl.pallas_call(
            body,
            out_shape=out_shape,
            grid_spec=pltpu.PrefetchScalarGridSpec(
                num_scalar_prefetch=1,
                grid=grid,
                in_specs=in_specs,
                out_specs=out_specs,
                scratch_shapes=scratch,
            ),
            input_output_aliases=aliases,
            compiler_params=params_of(60 << 20),
            cost_estimate=pl.CostEstimate(flops=cost, transcendentals=0, bytes_accessed=cost // 200),
        )(me, *operands)

    spread = jnp.asarray(table["spread"])
    spread_spec = pl.BlockSpec((128, BLOCK), lambda i, m: (0, i % quarters))

    def front(chunk, after):
        moment, moment_spec = tab("moment")
        final = chunk == CHUNKS - 1
        mom_spec = pl.BlockSpec((32, BLOCK), lambda i, m: (0, i))
        in_specs = [wide(chunk)] * 4 + [
            pl.BlockSpec((24, BLOCK), lambda i, m: (0, i)), shorts(chunk), moment_spec, spread_spec,
        ]
        operands = [query, key, value, grad_out, rims[chunk], short_all, moment, spread]
        out_shape = (part,) * 5 + (
            jax.ShapeDtypeStruct((32, per), F32), jax.ShapeDtypeStruct((24, per), F32),
        )
        out_specs = (here,) * 5 + (mom_spec, pl.BlockSpec((24, BLOCK), lambda i, m: (0, i)))
        if final:
            in_specs += [mom_spec] * chunk + [poles_at(c, 0) for c in range(CHUNKS)]
            operands += [f[5] for f in fronts] + [poles_all] * CHUNKS
            out_shape += (jax.ShapeDtypeStruct((2, CHUNKS, per // 128, 8, 128), BF16),)
            out_specs += (
                pl.BlockSpec((2, CHUNKS, group, 8, 128), lambda i, m: (0, 0, i, 0, 0)),
            )
        return call(
            functools.partial(front_kernel, pieces=CHUNKS if final else 0),
            2_000_000_000, (steps,), in_specs, operands, out_shape, out_specs,
            [pltpu.VMEM((group, rows + 8, 128), F32)] * 3,
            after=after,
        )

    fronts, behinds, aheads = [], [], []

    def exchange(chunk, after):
        prod, gconv, after = lax.optimization_barrier((fronts[chunk][3], fronts[chunk][4], after))
        behinds.append(shift(prod, 1))
        aheads.append(shift(gconv, -1))
        return after

    fronts.append(front(0, []))
    poles_all = jnp.stack(exchange(0, tuple(poles_parts)))
    for chunk in range(1, CHUNKS):
        fronts.append(front(chunk, [fronts[-1][5]]))
    states = fronts[-1][7].reshape(2 * half, 8, 128)
    arrived = lax.all_to_all(states, AXES, 0, 0, tiled=True)
    for chunk in range(1, CHUNKS):
        exchange(chunk, states)
    ctxs = lax.axis_size("ctx")
    share = rows // ctxs

    def mid(chunk, pieces, after):
        consts = [tab(name) for name in ("own", "before", "after", "taps", "head", "inverse3")]
        spec32 = pltpu.VMEM((2 * rows, BLOCK), F32)
        spec16 = pltpu.VMEM((2 * rows, BLOCK), BF16)
        return call(
            mid_kernel, 2_000_000_000, (steps,),
            [here] * 4
            + [
                poles_at(chunk, 0),
                poles_at(chunk, quarters),
                pl.BlockSpec((1, 128, 128), lambda i, m: (owned(chunk, i, m), 2, 0)),
            ]
            + [spec for _, spec in consts]
            + [spread_spec]
            + [pl.BlockSpec(memory_space=pl.ANY)] * len(pieces),
            [fronts[chunk][3], fronts[chunk][4], behinds[chunk], aheads[chunk]]
            + [poles_all] * 3
            + [c for c, _ in consts]
            + [spread]
            + pieces,
            (spectrum,) * 2 + (jax.ShapeDtypeStruct((ctxs, owners, share, 128), F32),),
            (bins,) * 2
            + (
                pl.BlockSpec(
                    (ctxs, 1, share, 128),
                    lambda i, m: (0, chunk * (owners // CHUNKS) + i // quarters, 0, 0),
                ),
            ),
            [spec16]
            + [spec32] * 6
            + [
                spec16,
                pltpu.VMEM((2 * rows, 256), BF16),
                pltpu.VMEM((2 * rows, 128), F32),
                pltpu.VMEM((16, BLOCK), F32),
            ],
            {8 + len(consts) + 1: 2} if pieces else {},
            after,
        )

    def back(chunk, ys, zs, outs, after):
        consts = [tab(name) for name in ("inverse", "ahead", "behind")]
        made = fronts[chunk]
        operands = [
            made[0], made[1], made[2], grad_out, ys, zs, carried, carried,
            made[6], poles_all, poles_all,
        ] + [c for c, _ in consts]
        in_specs = [
            here, here, here, wide(chunk), bins, bins,
            pl.BlockSpec((group, 8, 128), lambda i, m: (chunk * steps + i, 0, 0)),
            pl.BlockSpec((group, 8, 128), lambda i, m: ((CHUNKS + chunk) * steps + i, 0, 0)),
            pl.BlockSpec((24, BLOCK), lambda i, m: (0, i)),
            poles_at(chunk, 0),
            poles_at(chunk, quarters),
        ] + [spec for _, spec in consts]
        aliases = {}
        for at, out in enumerate(outs):
            aliases[1 + len(operands)] = at
            operands.append(out)
            in_specs.append(pl.BlockSpec(memory_space=pl.ANY))
        ext = pltpu.VMEM((group, rows + 8, 128), F32)
        plain = pltpu.VMEM((rows, BLOCK), F32)
        return call(
            back_kernel, 2_000_000_000, (steps,), in_specs, operands,
            (full,) * 4
            + (jax.ShapeDtypeStruct((24, per), BF16), jax.ShapeDtypeStruct((24, per), F32)),
            (wide(chunk),) * 4
            + (
                pl.BlockSpec((24, BLOCK), lambda i, m: (0, i)),
                pl.BlockSpec((24, BLOCK), lambda i, m: (0, i)),
            ),
            [ext, ext, ext, pltpu.VMEM((32, BLOCK), F32), plain, plain],
            aliases,
            after,
        )

    mids = [mid(0, [], [])]
    scanned = call(
        scan_kernel, 200_000_000, (1,),
        [
            whole(arrived.shape),
            pl.BlockSpec(
                (1, 8, 128),
                lambda i, m: (
                    (m[0] - m[2] // (half // owners) + owners) % owners, m[2] % (half // owners), 0
                ),
            ),
        ],
        (arrived, poles_all),
        jax.ShapeDtypeStruct(arrived.shape, BF16),
        whole(arrived.shape),
        [],
        after=[mids[0][2]],
    )
    carried = lax.all_to_all(scanned, AXES, 0, 0, tiled=True)

    outs, edges, lasts = (), [], []

    def finish(chunk, after):
        made = back(chunk, mids[chunk][0], mids[chunk][1], outs, after)
        edges.append(shift(made[4], -1))
        lasts.append(made[5])
        return made[:4]

    for chunk in range(1, CHUNKS):
        mids.append(mid(chunk, [mids[-1][2]], [scanned]))
    landed = lax.all_to_all(mids[-1][2].reshape(ctxs * owners, share, 128), AXES, 0, 0, tiled=True)
    for chunk in range(CHUNKS):
        outs = finish(chunk, [])
    tokens = rows * ctxs * owners
    total = landed.sum(axis=0) * (1.0 / math.sqrt(tokens * CPG))
    every = lax.all_to_all(
        jnp.broadcast_to(total[None], (ctxs, share, 128)), "ctx", 0, 0, tiled=True
    )

    cuts = 1
    strip = pl.BlockSpec((8, per // cuts), lambda i, m: (rows // 8 - 1, i))
    bands = [
        pl.BlockSpec(
            (24, per // cuts),
            lambda i, m, chunk=chunk: (0, jnp.clip(i - cuts * chunk, 0, cuts - 1)),
        )
        for chunk in range(CHUNKS)
    ]
    anyspec = pl.BlockSpec(memory_space=pl.ANY)
    grads = call(
        tail_kernel, 200_000_000, (CHUNKS * cuts,),
        bands * 3 + [anyspec] * 3,
        (*lasts, *edges, *[f[6] for f in fronts], *outs[1:4]),
        (full,) * 3,
        (strip,) * 3,
        [pltpu.VMEM((3, 16, 128), F32)],
        {3 * CHUNKS + 1: 0, 3 * CHUNKS + 2: 1, 3 * CHUNKS + 3: 2},
    )
    return (outs[0],) + tuple(grads) + (every.reshape(rows, 128),)


def solution(mesh):
    placed = (
        P(AXES, None),
        P(AXES, None),
        P(AXES, None),
        P(None, None, "own"),
        P(None, "own"),
        P(None, "own"),
        P(None, "own"),
        P(AXES, None),
    )
    return jax.shard_map(
        shards,
        mesh=mesh,
        in_specs=placed,
        out_specs=(P(AXES, None),) * 4 + (P(None, "own"),),
        check_vma=False,
    )
```

```python
import functools
import math

import jax
import jax.numpy as jnp
import numpy as np
from jax import lax
from jax.experimental import pallas as pl
from jax.experimental.pallas import tpu as pltpu
from jax.sharding import PartitionSpec as P

CPG = 16
BLOCK = 512
CHUNKS = 2
TERMS = 16
RATE_TOP = 0.03
AXES = ("ctx", "own")
F32, BF16 = jnp.float32, jnp.bfloat16


def split_np(table):
    high = table.astype(np.float32).astype(jnp.bfloat16)
    low = (table - high.astype(np.float64)).astype(np.float32).astype(jnp.bfloat16)
    return high, low


def series(lags):
    nodes = np.cos(np.pi * (np.arange(64) + 0.5) / 64)
    values = np.exp(-np.outer(np.asarray(lags, np.float64), RATE_TOP / 2 * (1 + nodes)))
    basis = np.cos(np.outer(np.arange(TERMS), np.pi * (np.arange(64) + 0.5) / 64))
    coeff = values @ basis.T * (2.0 / 64)
    coeff[:, 0] *= 0.5
    return coeff


def tables(rows):
    angle = np.pi * (2 * np.arange(rows) + 1) / (2 * rows)

    def forward(places):
        phase = np.outer(angle, places)
        return np.concatenate([np.cos(phase), -np.sin(phase)])

    here = np.arange(rows)
    own, before, after = forward(here), forward(here - rows), forward(here + rows)
    phase = np.outer(here, angle)
    inverse = np.concatenate([np.cos(phase), -np.sin(phase)], axis=1) / rows
    cat = np.concatenate
    pair = lambda m: cat(split_np(m), axis=1)

    def triple(m):
        high, low = split_np(m)
        return cat([high, low, high], axis=1)

    return dict(
        own=pair(own),
        before=pair(before),
        after=pair(after),
        taps=triple(own),
        head=triple(own @ series(here)),
        inverse=split_np(inverse)[0],
        inverse3=triple(inverse),
        ahead=triple(series(here + 1)),
        behind=triple(series(rows - here)),
        spread=(np.arange(16 * rows)[None, :] // CPG == here[:, None]).astype(jnp.bfloat16),
        moment=cat(
            [
                pair(series(rows - 1 - here).T),
                pair(series(here).T),
            ],
            axis=0,
        ),
    )


def dot(a, b):
    return jnp.dot(a, b, preferred_element_type=F32)


def halves(x):
    high = x.astype(BF16)
    return high, (x - high.astype(F32)).astype(BF16)


def stack3(x):
    high, low = halves(x)
    return jnp.concatenate([high, high, low], axis=0)


def spread_taps(short, spread):
    high, _ = halves(short)
    rest = short - high.astype(F32)
    mid, low = halves(rest)
    made = dot(jnp.concatenate([high, mid, low], axis=0), spread)
    return made[0:24] + made[24:48] + made[48:72]


def chebyshev(rate):
    z = rate * (2.0 / RATE_TOP) - 1.0
    terms = [jnp.ones_like(z), z]
    while len(terms) < TERMS:
        terms.append(2.0 * z * terms[-1] - terms[-2])
    return terms


def pack_kernel(q, k, v, short, rate, resid, ltaps, small, big, *rims):
    for chunk, rim in enumerate(rims):
        for at, src in enumerate((q, k, v)):
            rim[8 * at : 8 * at + 8] = src[:, rim.shape[1] * chunk : rim.shape[1] * (chunk + 1)]
    small[...] = jnp.zeros_like(small)
    for at in range(3):
        small[7 * at : 7 * at + 7] = short[at]
    for tile in range(rate.shape[1] // 128):
        cols = slice(128 * tile, 128 * tile + 128)
        big[8 * tile : 8 * tile + 8] = rate[:, cols]
        big[128 + 8 * tile : 136 + 8 * tile] = resid[:, cols]
    big[256:] = ltaps[...]


def front_kernel(
    me, q, k, v, g, rim, short, moment, spread, *rest, pieces=0
):
    moms, rates = rest[: max(pieces - 1, 0)], rest[max(pieces - 1, 0) : max(2 * pieces - 1, 0)]
    outs = rest[len(moms) + len(rates) :]
    qf, kf, vf, prod, gconv, mom, taps = outs[:7]
    xq, xk, xv = outs[-3:]
    rows = q.shape[0]
    taps[...] = spread_taps(short[0], spread[...])
    lanes = range(BLOCK // 128)
    for at, (src, dst) in enumerate(((q, xq), (k, xk), (v, xv))):
        for lane in lanes:
            cols = slice(128 * lane, 128 * lane + 128)
            dst[lane, 0:8] = rim[8 * at : 8 * at + 8, cols].astype(F32)
            dst[lane, 8:] = src[:, cols].astype(F32)

    def step(r, _):
        base = pl.multiple_of(r * 32, 32)
        here = pl.ds(base, 32)
        for lane in lanes:
            cols = slice(128 * lane, 128 * lane + 128)
            feats = []
            for at, src in enumerate((xq, xk, xv)):
                total = taps[7 * at : 7 * at + 1, cols] * src[lane, pl.ds(base + 8, 32), :]
                for j in range(1, 7):
                    tap = taps[7 * at + j : 7 * at + j + 1, cols]
                    total = total + tap * src[lane, pl.ds(base + 8 - j, 32), :]
                feats.append(total.astype(BF16))
            qf[here, cols] = feats[0]
            kf[here, cols] = feats[1]
            vf[here, cols] = feats[2]
            prod[here, cols] = (feats[1].astype(F32) * feats[2].astype(F32)).astype(BF16)
            gconv[here, cols] = (g[here, cols].astype(F32) * feats[0].astype(F32)).astype(BF16)
        return 0

    lax.fori_loop(0, rows // 32, step, 0)
    p, c = prod[...], gconv[...]
    mom[0:16] = dot(moment[0:16, :], jnp.concatenate([p, p], axis=0))
    mom[16:32] = dot(moment[16:32, :], jnp.concatenate([c, c], axis=0))
    for piece in range(pieces):
        source, states = (*moms, mom)[piece], outs[7]
        for lane in lanes:
            mine = source[:, 128 * lane : 128 * lane + 128]
            terms = chebyshev(rates[piece][0, 8 * lane : 8 * lane + 8, :])
            ahead = terms[0] * mine[0:1]
            back = terms[0] * mine[16:17]
            for at in range(1, TERMS):
                ahead = ahead + terms[at] * mine[at : at + 1]
                back = back + terms[at] * mine[16 + at : 17 + at]
            states[0, piece, lane] = ahead.astype(BF16)
            states[1, piece, lane] = back.astype(BF16)


def scan_kernel(me, states, rates, out):
    count = states.shape[0]
    backward = me[1]
    factor = jnp.exp(rates[0] * -128.0)

    def hop(n, carry):
        at = jnp.where(backward == 1, count - 1 - n, n)
        out[at] = carry.astype(BF16)
        return factor * carry + states[at].astype(F32)

    lax.fori_loop(0, count, hop, jnp.zeros((8, 128), F32), unroll=8)


def modal_weight(rate, resid):
    x = 2.0 * rate
    return resid * jnp.sqrt(x * modal_series(x))


def modal_series(x):
    total = 1.0 - x * (1.0 / 8)
    for n in (7, 6, 5, 4, 3, 2):
        total = 1.0 - x * (1.0 / n) * total
    return total


def mid_kernel(
    me, prod, gconv, before, after, rates, resids, ltaps,
    t_own, t_before, t_after, t_taps, t_head, t_inv3, spread,
    *rest,
):
    (yout, zout, tgrad, xx, own, prv, cur, nxt, tre, hre, cs, tsp, acc, coef) = rest[-14:]
    rows = prod.shape[0]
    quarter = pl.program_id(0) % (128 * CPG // BLOCK)

    @pl.when(quarter == 0)
    def _():
        spec = dot(t_taps[...], stack3(ltaps[0]))
        high, low = halves(spec)
        tsp[:, 0:128] = high
        tsp[:, 128:256] = low
        acc[...] = jnp.zeros_like(acc)

    one_hot = spread[...]
    xx[0:128] = one_hot
    xx[128:256] = one_hot
    for lane in range(BLOCK // 128):
        cols = slice(128 * lane, 128 * lane + 128)
        eight = slice(8 * lane, 8 * lane + 8)
        weight = modal_weight(rates[0, eight, :], resids[0, eight, :])
        for n, term in enumerate(chebyshev(rates[0, eight, :])):
            coef[n : n + 1, cols] = jnp.sum(term * weight, axis=0, keepdims=True)

    def transforms(half):
        wide = slice(256 * half, 256 * half + 256)
        tre[:, wide] = dot(tsp[...], xx[:, wide])
        for src, table, dst in (
            (prod, t_own, own), (before, t_before, prv), (gconv, t_own, cur), (after, t_after, nxt),
        ):
            value = src[:, wide]
            dst[:, wide] = dot(table[...], jnp.concatenate([value, value], axis=0))
        hre[:, wide] = dot(t_head[...], stack3(coef[:, wide]))

    def bins(base, lane):
        re = slice(base, base + 16)
        im = slice(rows + base, rows + base + 16)
        cols = slice(128 * lane, 128 * lane + 128)
        tr, ti, hr, hi = tre[re, cols], tre[im, cols], hre[re, cols], hre[im, cols]
        pr, pi, cr, ci = own[re, cols], own[im, cols], cur[re, cols], cur[im, cols]
        wr, wi = pr + prv[re, cols], pi + prv[im, cols]
        ar, ai = cr + nxt[re, cols], ci + nxt[im, cols]
        yout[re, cols] = (wr * tr - wi * ti + (pr * hr - pi * hi)).astype(BF16)
        yout[im, cols] = (wr * ti + wi * tr + (pr * hi + pi * hr)).astype(BF16)
        zout[re, cols] = (ar * tr + ai * ti + (cr * hr + ci * hi)).astype(BF16)
        zout[im, cols] = (ai * tr - ar * ti + (ci * hr - cr * hi)).astype(BF16)
        cs[re, cols] = (cr * wr + ci * wi).astype(BF16)
        cs[im, cols] = (ci * wr - cr * wi).astype(BF16)

    for half in range(BLOCK // 256):
        transforms(half)
        for lane in (2 * half, 2 * half + 1):
            for base in range(0, rows, 16):
                bins(base, lane)
    acc[...] += lax.dot_general(
        cs[...], spread[...], (((1,), (1,)), ((), ())), preferred_element_type=F32
    )

    @pl.when(quarter == 128 * CPG // BLOCK - 1)
    def _():
        made = dot(t_inv3[...], stack3(acc[...]))
        share = tgrad.shape[2]
        for at in range(tgrad.shape[0]):
            tgrad[at, 0] = made[share * at : share * at + share]


def back_kernel(
    me, qf, kf, vf, g, ys, zs, sf, sb, taps, rates, resids,
    t_inv, t_ahead, t_behind, *rest,
):
    (layer, gq, gk, gv, rim, last, eq, ek, ev, coef, lg, gp) = rest[-12:]
    rows = qf.shape[0]
    lanes = range(BLOCK // 128)
    for lane in lanes:
        cols = slice(128 * lane, 128 * lane + 128)
        eight = slice(8 * lane, 8 * lane + 8)
        weight = modal_weight(rates[0, eight, :], resids[0, eight, :])
        sets = (weight * sf[lane].astype(F32), weight * sb[lane].astype(F32))
        for n, term in enumerate(chebyshev(rates[0, eight, :])):
            for at, field in enumerate(sets):
                coef[16 * at + n : 16 * at + n + 1, cols] = jnp.sum(
                    term * field, axis=0, keepdims=True
                )
    lg[...] = dot(t_inv[...], ys[...]) + dot(t_ahead[...], stack3(coef[0:16]))
    gp[...] = dot(t_inv[...], zs[...]) + dot(t_behind[...], stack3(coef[16:32]))

    for base in range(0, rows, 16):
        here = slice(base, base + 16)
        for lane in lanes:
            cols = slice(128 * lane, 128 * lane + 128)
            conv, grad = lg[here, cols], gp[here, cols]
            layer[here, cols] = (qf[here, cols].astype(F32) * conv).astype(BF16)
            eq[lane, here] = (g[here, cols].astype(F32) * conv).astype(BF16).astype(F32)
            ek[lane, here] = (grad * vf[here, cols].astype(F32)).astype(BF16).astype(F32)
            ev[lane, here] = (grad * kf[here, cols].astype(F32)).astype(BF16).astype(F32)
    for at, src in enumerate((eq, ek, ev)):
        for lane in lanes:
            cols = slice(128 * lane, 128 * lane + 128)
            src[lane, rows:] = jnp.zeros((8, 128), F32)
            rim[8 * at : 8 * at + 8, cols] = src[lane, 0:8].astype(BF16)

    def finish(r, _):
        base = pl.multiple_of(r * 32, 32)
        here = pl.ds(base, 32)
        for lane in lanes:
            cols = slice(128 * lane, 128 * lane + 128)
            for at, (src, dst) in enumerate(((eq, gq), (ek, gk), (ev, gv))):
                total = taps[7 * at : 7 * at + 1, cols] * src[lane, here, :]
                for j in range(1, 7):
                    tap = taps[7 * at + j : 7 * at + j + 1, cols]
                    total = total + tap * src[lane, pl.ds(base + j, 32), :]
                dst[here, cols] = total.astype(BF16)
                last[8 * at : 8 * at + 8, cols] = total[24:32]
        return 0

    lax.fori_loop(0, rows // 32, finish, 0)


def tail_kernel(me, last, rim, tap, gq_in, gk_in, gv_in, gq, gk, gv, ext):
    ext[:, 0:8] = jnp.zeros((3, 8, 128), F32)

    def tile(n, _):
        cols = pl.ds(pl.multiple_of(n * 128, 128), 128)
        for at, dst in enumerate((gq, gk, gv)):
            ext[at, 8:16] = rim[8 * at : 8 * at + 8, cols].astype(F32)
            total = last[8 * at : 8 * at + 8, cols]
            for j in range(1, 7):
                total = total + tap[7 * at + j : 7 * at + j + 1, cols] * ext[at, j : 8 + j]
            dst[:, cols] = total.astype(BF16)
        return 0

    lax.fori_loop(0, last.shape[1] // 128, tile, 0, unroll=4)


def shift(value, steps):
    count = lax.axis_size(AXES)
    first, last = max(0, -steps), min(count, count - steps)
    return lax.ppermute(value, AXES, [(at, at + steps) for at in range(first, last)])


def gather_own(value):
    return jnp.stack(ring_own(value))


def ring_own(value):
    count = lax.axis_size("own")
    parts = [value]
    for hop in range(1, count):
        parts.append(lax.ppermute(value, "own", [(at, (at + hop) % count) for at in range(count)]))
    return parts


def params_of(vmem):
    return pltpu.CompilerParams(
        dimension_semantics=("arbitrary",), vmem_limit_bytes=vmem
    )


def shards(query, key, value, short_taps, long_taps, decay_rate, residues, grad_out):
    rows, width = query.shape
    owners = lax.axis_size("own")
    per = width // CHUNKS
    steps = per // BLOCK
    quarters = width // owners // BLOCK
    ctx, own = lax.axis_index("ctx"), lax.axis_index("own")
    flat = ctx * owners + own
    half = width // 128
    me = jnp.stack([own, flat // half, flat % half]).astype(jnp.int32)
    table = tables(rows)
    group = BLOCK // 128
    whole = lambda shape: pl.BlockSpec(shape, lambda i, *m: (0,) * len(shape))
    edge = pl.BlockSpec((8, width), lambda i: (rows // 8 - 1, 0))

    short, poles, *rims = pl.pallas_call(
        pack_kernel,
        out_shape=(
            jax.ShapeDtypeStruct((24, 128), F32),
            jax.ShapeDtypeStruct((384, 128), F32),
        )
        + (jax.ShapeDtypeStruct((24, per), BF16),) * CHUNKS,
        grid=(1,),
        in_specs=[edge] * 3
        + [whole(short_taps.shape), whole(decay_rate.shape), whole(residues.shape), whole(long_taps.shape)],
        out_specs=(
            whole((24, 128)),
            whole((384, 128)),
        )
        + (whole((24, per)),) * CHUNKS,
        compiler_params=params_of(60 << 20),
        name="pack",
    )(query, key, value, short_taps, decay_rate, residues, long_taps)
    rims[0] = shift(rims[0], 1)
    short_all = gather_own(short)
    poles_parts = ring_own(poles)
    for chunk in range(1, CHUNKS):
        edge_rows, _ = lax.optimization_barrier((rims[chunk], short_all))
        rims[chunk] = shift(edge_rows, 1)

    def slot(me_ref, chunk):
        return (me_ref[0] - chunk + owners) % owners

    tab = lambda name: (jnp.asarray(table[name]), whole(table[name].shape))
    full = jax.ShapeDtypeStruct((rows, width), BF16)
    part = jax.ShapeDtypeStruct((rows, per), BF16)
    spectrum = jax.ShapeDtypeStruct((2 * rows, per), BF16)
    here = pl.BlockSpec((rows, BLOCK), lambda i, m: (0, i))
    bins = pl.BlockSpec((2 * rows, BLOCK), lambda i, m: (0, i))

    def wide(chunk):
        return pl.BlockSpec((rows, BLOCK), lambda i, m: (0, chunk * steps + i))

    def owned(chunk, i, me_ref):
        return slot(me_ref, chunk * (owners // CHUNKS) + i // quarters)

    def shorts(chunk):
        return pl.BlockSpec((1, 24, 128), lambda i, m: (owned(chunk, i, m), 0, 0))

    def poles_at(chunk, first):
        return pl.BlockSpec(
            (1, 8 * group, 128), lambda i, m: (owned(chunk, i, m), first + i % quarters, 0)
        )

    def call(
        kernel, cost, grid, in_specs, operands, out_shape, out_specs, scratch,
        aliases={}, after=(),
    ):
        known = 1 + len(operands)

        def body(*refs):
            kernel(*refs[:known], *refs[known + len(after) :])

        in_specs = list(in_specs) + [pl.BlockSpec(memory_space=pl.ANY)] * len(after)
        operands = list(operands) + list(after)
        return pl.pallas_call(
            body,
            out_shape=out_shape,
            grid_spec=pltpu.PrefetchScalarGridSpec(
                num_scalar_prefetch=1,
                grid=grid,
                in_specs=in_specs,
                out_specs=out_specs,
                scratch_shapes=scratch,
            ),
            input_output_aliases=aliases,
            compiler_params=params_of(60 << 20),
            cost_estimate=pl.CostEstimate(flops=cost, transcendentals=0, bytes_accessed=cost // 200),
        )(me, *operands)

    spread = jnp.asarray(table["spread"])
    spread_spec = pl.BlockSpec((128, BLOCK), lambda i, m: (0, i % quarters))

    def front(chunk, after):
        moment, moment_spec = tab("moment")
        final = chunk == CHUNKS - 1
        mom_spec = pl.BlockSpec((32, BLOCK), lambda i, m: (0, i))
        in_specs = [wide(chunk)] * 4 + [
            pl.BlockSpec((24, BLOCK), lambda i, m: (0, i)), shorts(chunk), moment_spec, spread_spec,
        ]
        operands = [query, key, value, grad_out, rims[chunk], short_all, moment, spread]
        out_shape = (part,) * 5 + (
            jax.ShapeDtypeStruct((32, per), F32), jax.ShapeDtypeStruct((24, per), F32),
        )
        out_specs = (here,) * 5 + (mom_spec, pl.BlockSpec((24, BLOCK), lambda i, m: (0, i)))
        if final:
            in_specs += [mom_spec] * chunk + [poles_at(c, 0) for c in range(CHUNKS)]
            operands += [f[5] for f in fronts] + [poles_all] * CHUNKS
            out_shape += (jax.ShapeDtypeStruct((2, CHUNKS, per // 128, 8, 128), BF16),)
            out_specs += (
                pl.BlockSpec((2, CHUNKS, group, 8, 128), lambda i, m: (0, 0, i, 0, 0)),
            )
        return call(
            functools.partial(front_kernel, pieces=CHUNKS if final else 0),
            2_000_000_000, (steps,), in_specs, operands, out_shape, out_specs,
            [pltpu.VMEM((group, rows + 8, 128), F32)] * 3,
            after=after,
        )

    fronts, behinds, aheads = [], [], []

    def exchange(chunk, after):
        prod, gconv, after = lax.optimization_barrier((fronts[chunk][3], fronts[chunk][4], after))
        behinds.append(shift(prod, 1))
        aheads.append(shift(gconv, -1))
        return after

    fronts.append(front(0, []))
    poles_all = jnp.stack(exchange(0, tuple(poles_parts)))
    for chunk in range(1, CHUNKS):
        fronts.append(front(chunk, [fronts[-1][5]]))
    states = fronts[-1][7].reshape(2 * half, 8, 128)
    arrived = lax.all_to_all(states, AXES, 0, 0, tiled=True)
    for chunk in range(1, CHUNKS):
        exchange(chunk, states)
    ctxs = lax.axis_size("ctx")
    share = rows // ctxs

    def mid(chunk, pieces, after):
        consts = [tab(name) for name in ("own", "before", "after", "taps", "head", "inverse3")]
        spec32 = pltpu.VMEM((2 * rows, BLOCK), F32)
        spec16 = pltpu.VMEM((2 * rows, BLOCK), BF16)
        return call(
            mid_kernel, 2_000_000_000, (steps,),
            [here] * 4
            + [
                poles_at(chunk, 0),
                poles_at(chunk, quarters),
                pl.BlockSpec((1, 128, 128), lambda i, m: (owned(chunk, i, m), 2, 0)),
            ]
            + [spec for _, spec in consts]
            + [spread_spec]
            + [pl.BlockSpec(memory_space=pl.ANY)] * len(pieces),
            [fronts[chunk][3], fronts[chunk][4], behinds[chunk], aheads[chunk]]
            + [poles_all] * 3
            + [c for c, _ in consts]
            + [spread]
            + pieces,
            (spectrum,) * 2 + (jax.ShapeDtypeStruct((ctxs, owners, share, 128), F32),),
            (bins,) * 2
            + (
                pl.BlockSpec(
                    (ctxs, 1, share, 128),
                    lambda i, m: (0, chunk * (owners // CHUNKS) + i // quarters, 0, 0),
                ),
            ),
            [spec16]
            + [spec32] * 6
            + [
                spec16,
                pltpu.VMEM((2 * rows, 256), BF16),
                pltpu.VMEM((2 * rows, 128), F32),
                pltpu.VMEM((16, BLOCK), F32),
            ],
            {8 + len(consts) + 1: 2} if pieces else {},
            after,
        )

    def back(chunk, ys, zs, outs, after):
        consts = [tab(name) for name in ("inverse", "ahead", "behind")]
        made = fronts[chunk]
        operands = [
            made[0], made[1], made[2], grad_out, ys, zs, carried, carried,
            made[6], poles_all, poles_all,
        ] + [c for c, _ in consts]
        in_specs = [
            here, here, here, wide(chunk), bins, bins,
            pl.BlockSpec((group, 8, 128), lambda i, m: (chunk * steps + i, 0, 0)),
            pl.BlockSpec((group, 8, 128), lambda i, m: ((CHUNKS + chunk) * steps + i, 0, 0)),
            pl.BlockSpec((24, BLOCK), lambda i, m: (0, i)),
            poles_at(chunk, 0),
            poles_at(chunk, quarters),
        ] + [spec for _, spec in consts]
        aliases = {}
        for at, out in enumerate(outs):
            aliases[1 + len(operands)] = at
            operands.append(out)
            in_specs.append(pl.BlockSpec(memory_space=pl.ANY))
        ext = pltpu.VMEM((group, rows + 8, 128), F32)
        plain = pltpu.VMEM((rows, BLOCK), F32)
        return call(
            back_kernel, 2_000_000_000, (steps,), in_specs, operands,
            (full,) * 4
            + (jax.ShapeDtypeStruct((24, per), BF16), jax.ShapeDtypeStruct((24, per), F32)),
            (wide(chunk),) * 4
            + (
                pl.BlockSpec((24, BLOCK), lambda i, m: (0, i)),
                pl.BlockSpec((24, BLOCK), lambda i, m: (0, i)),
            ),
            [ext, ext, ext, pltpu.VMEM((32, BLOCK), F32), plain, plain],
            aliases,
            after,
        )

    mids = [mid(0, [], [])]
    scanned = call(
        scan_kernel, 200_000_000, (1,),
        [
            whole(arrived.shape),
            pl.BlockSpec(
                (1, 8, 128),
                lambda i, m: (
                    (m[0] - m[2] // (half // owners) + owners) % owners, m[2] % (half // owners), 0
                ),
            ),
        ],
        (arrived, poles_all),
        jax.ShapeDtypeStruct(arrived.shape, BF16),
        whole(arrived.shape),
        [],
        after=[mids[0][2]],
    )
    carried = lax.all_to_all(scanned, AXES, 0, 0, tiled=True)

    outs, edges, lasts = (), [], []

    def finish(chunk, after):
        made = back(chunk, mids[chunk][0], mids[chunk][1], outs, after)
        edges.append(shift(made[4], -1))
        lasts.append(made[5])
        return made[:4]

    for chunk in range(1, CHUNKS):
        mids.append(mid(chunk, [mids[-1][2]], [scanned]))
    landed = lax.all_to_all(mids[-1][2].reshape(ctxs * owners, share, 128), AXES, 0, 0, tiled=True)
    for chunk in range(CHUNKS):
        outs = finish(chunk, [])
    tokens = rows * ctxs * owners
    total = landed.sum(axis=0) * (1.0 / math.sqrt(tokens * CPG))
    every = lax.all_to_all(
        jnp.broadcast_to(total[None], (ctxs, share, 128)), "ctx", 0, 0, tiled=True
    )

    every = every.reshape(rows, 128)
    grads = outs[1:4]
    for chunk in range(CHUNKS):
        grads = call(
            tail_kernel, 200_000_000, (1,),
            [whole((24, per))] * 3 + [pl.BlockSpec(memory_space=pl.ANY)] * 3,
            (lasts[chunk], edges[chunk], fronts[chunk][6], *grads),
            (full,) * 3,
            (pl.BlockSpec((8, per), lambda i, m, chunk=chunk: (rows // 8 - 1, chunk)),) * 3,
            [pltpu.VMEM((3, 16, 128), F32)],
            {4: 0, 5: 1, 6: 2},
            [every] if chunk == CHUNKS - 1 else [],
        )
    return (outs[0],) + tuple(grads) + (every,)


def solution(mesh):
    placed = (
        P(AXES, None),
        P(AXES, None),
        P(AXES, None),
        P(None, None, "own"),
        P(None, "own"),
        P(None, "own"),
        P(None, "own"),
        P(AXES, None),
    )
    return jax.shard_map(
        shards,
        mesh=mesh,
        in_specs=placed,
        out_specs=(P(AXES, None),) * 4 + (P(None, "own"),),
        check_vma=False,
    )
```

```python
import functools
import math

import jax
import jax.numpy as jnp
import numpy as np
from jax import lax
from jax.experimental import pallas as pl
from jax.experimental.pallas import tpu as pltpu
from jax.sharding import PartitionSpec as P

CPG = 16
BLOCK = 512
CHUNKS = 2
TERMS = 16
RATE_TOP = 0.03
AXES = ("ctx", "own")
F32, BF16 = jnp.float32, jnp.bfloat16


def split_np(table):
    high = table.astype(np.float32).astype(jnp.bfloat16)
    low = (table - high.astype(np.float64)).astype(np.float32).astype(jnp.bfloat16)
    return high, low


def series(lags):
    nodes = np.cos(np.pi * (np.arange(64) + 0.5) / 64)
    values = np.exp(-np.outer(np.asarray(lags, np.float64), RATE_TOP / 2 * (1 + nodes)))
    basis = np.cos(np.outer(np.arange(TERMS), np.pi * (np.arange(64) + 0.5) / 64))
    coeff = values @ basis.T * (2.0 / 64)
    coeff[:, 0] *= 0.5
    return coeff


def tables(rows):
    angle = np.pi * (2 * np.arange(rows) + 1) / (2 * rows)

    def forward(places):
        phase = np.outer(angle, places)
        return np.concatenate([np.cos(phase), -np.sin(phase)])

    here = np.arange(rows)
    own, before, after = forward(here), forward(here - rows), forward(here + rows)
    phase = np.outer(here, angle)
    inverse = np.concatenate([np.cos(phase), -np.sin(phase)], axis=1) / rows
    cat = np.concatenate
    pair = lambda m: cat(split_np(m), axis=1)

    def triple(m):
        high, low = split_np(m)
        return cat([high, low, high], axis=1)

    return dict(
        own=pair(own),
        before=pair(before),
        after=pair(after),
        taps=triple(own),
        head=triple(own @ series(here)),
        inverse=split_np(inverse)[0],
        inverse3=triple(inverse),
        ahead=triple(series(here + 1)),
        behind=triple(series(rows - here)),
        spread=(np.arange(16 * rows)[None, :] // CPG == here[:, None]).astype(jnp.bfloat16),
        moment=cat(
            [
                pair(series(rows - 1 - here).T),
                pair(series(here).T),
            ],
            axis=0,
        ),
    )


def dot(a, b):
    return jnp.dot(a, b, preferred_element_type=F32)


def halves(x):
    high = x.astype(BF16)
    return high, (x - high.astype(F32)).astype(BF16)


def stack3(x):
    high, low = halves(x)
    return jnp.concatenate([high, high, low], axis=0)


def spread_taps(short, spread):
    high, _ = halves(short)
    rest = short - high.astype(F32)
    mid, low = halves(rest)
    made = dot(jnp.concatenate([high, mid, low], axis=0), spread)
    return made[0:24] + made[24:48] + made[48:72]


def chebyshev(rate):
    z = rate * (2.0 / RATE_TOP) - 1.0
    terms = [jnp.ones_like(z), z]
    while len(terms) < TERMS:
        terms.append(2.0 * z * terms[-1] - terms[-2])
    return terms


def pack_kernel(q, k, v, short, rate, resid, ltaps, small, big, *rims):
    for chunk, rim in enumerate(rims):
        for at, src in enumerate((q, k, v)):
            rim[8 * at : 8 * at + 8] = src[:, rim.shape[1] * chunk : rim.shape[1] * (chunk + 1)]
    small[...] = jnp.zeros_like(small)
    for at in range(3):
        small[7 * at : 7 * at + 7] = short[at]
    for tile in range(rate.shape[1] // 128):
        cols = slice(128 * tile, 128 * tile + 128)
        big[8 * tile : 8 * tile + 8] = rate[:, cols]
        big[128 + 8 * tile : 136 + 8 * tile] = resid[:, cols]
    big[256:] = ltaps[...]


def front_kernel(
    me, q, k, v, g, rim, short, moment, spread, *rest, pieces=0
):
    moms, rates = rest[: max(pieces - 1, 0)], rest[max(pieces - 1, 0) : max(2 * pieces - 1, 0)]
    outs = rest[len(moms) + len(rates) :]
    qf, kf, vf, prod, gconv, mom, taps = outs[:7]
    xq, xk, xv = outs[-3:]
    rows = q.shape[0]
    taps[...] = spread_taps(short[0], spread[...])
    lanes = range(BLOCK // 128)
    for at, (src, dst) in enumerate(((q, xq), (k, xk), (v, xv))):
        for lane in lanes:
            cols = slice(128 * lane, 128 * lane + 128)
            dst[lane, 0:8] = rim[8 * at : 8 * at + 8, cols].astype(F32)
            dst[lane, 8:] = src[:, cols].astype(F32)

    def step(r, _):
        base = pl.multiple_of(r * 32, 32)
        here = pl.ds(base, 32)
        for lane in lanes:
            cols = slice(128 * lane, 128 * lane + 128)
            feats = []
            for at, src in enumerate((xq, xk, xv)):
                total = taps[7 * at : 7 * at + 1, cols] * src[lane, pl.ds(base + 8, 32), :]
                for j in range(1, 7):
                    tap = taps[7 * at + j : 7 * at + j + 1, cols]
                    total = total + tap * src[lane, pl.ds(base + 8 - j, 32), :]
                feats.append(total.astype(BF16))
            qf[here, cols] = feats[0]
            kf[here, cols] = feats[1]
            vf[here, cols] = feats[2]
            prod[here, cols] = (feats[1].astype(F32) * feats[2].astype(F32)).astype(BF16)
            gconv[here, cols] = (g[here, cols].astype(F32) * feats[0].astype(F32)).astype(BF16)
        return 0

    lax.fori_loop(0, rows // 32, step, 0)
    p, c = prod[...], gconv[...]
    mom[0:16] = dot(moment[0:16, :], jnp.concatenate([p, p], axis=0))
    mom[16:32] = dot(moment[16:32, :], jnp.concatenate([c, c], axis=0))
    for piece in range(pieces):
        source, states = (*moms, mom)[piece], outs[7]
        for lane in lanes:
            mine = source[:, 128 * lane : 128 * lane + 128]
            terms = chebyshev(rates[piece][0, 8 * lane : 8 * lane + 8, :])
            ahead = terms[0] * mine[0:1]
            back = terms[0] * mine[16:17]
            for at in range(1, TERMS):
                ahead = ahead + terms[at] * mine[at : at + 1]
                back = back + terms[at] * mine[16 + at : 17 + at]
            states[0, piece, lane] = ahead.astype(BF16)
            states[1, piece, lane] = back.astype(BF16)


def scan_kernel(me, states, rates, out):
    count = states.shape[0]
    backward = me[1]
    factor = jnp.exp(rates[0] * -128.0)

    def hop(n, carry):
        at = jnp.where(backward == 1, count - 1 - n, n)
        out[at] = carry.astype(BF16)
        return factor * carry + states[at].astype(F32)

    lax.fori_loop(0, count, hop, jnp.zeros((8, 128), F32), unroll=8)


def modal_weight(rate, resid):
    x = 2.0 * rate
    return resid * jnp.sqrt(x * modal_series(x))


def modal_series(x):
    total = 1.0 - x * (1.0 / 8)
    for n in (7, 6, 5, 4, 3, 2):
        total = 1.0 - x * (1.0 / n) * total
    return total


def mid_kernel(
    me, prod, gconv, before, after, rates, resids, ltaps,
    t_own, t_before, t_after, t_taps, t_head, t_inv3, spread,
    *rest,
):
    (yout, zout, tgrad, xx, own, prv, cur, nxt, tre, hre, cs, tsp, acc, coef) = rest[-14:]
    rows = prod.shape[0]
    quarter = pl.program_id(0) % (128 * CPG // BLOCK)

    @pl.when(quarter == 0)
    def _():
        spec = dot(t_taps[...], stack3(ltaps[0]))
        high, low = halves(spec)
        tsp[:, 0:128] = high
        tsp[:, 128:256] = low
        acc[...] = jnp.zeros_like(acc)

    one_hot = spread[...]
    xx[0:128] = one_hot
    xx[128:256] = one_hot
    for lane in range(BLOCK // 128):
        cols = slice(128 * lane, 128 * lane + 128)
        eight = slice(8 * lane, 8 * lane + 8)
        weight = modal_weight(rates[0, eight, :], resids[0, eight, :])
        for n, term in enumerate(chebyshev(rates[0, eight, :])):
            coef[n : n + 1, cols] = jnp.sum(term * weight, axis=0, keepdims=True)

    def transforms(half):
        wide = slice(256 * half, 256 * half + 256)
        tre[:, wide] = dot(tsp[...], xx[:, wide])
        for src, table, dst in (
            (prod, t_own, own), (before, t_before, prv), (gconv, t_own, cur), (after, t_after, nxt),
        ):
            value = src[:, wide]
            dst[:, wide] = dot(table[...], jnp.concatenate([value, value], axis=0))
        hre[:, wide] = dot(t_head[...], stack3(coef[:, wide]))

    def bins(base, lane):
        re = slice(base, base + 16)
        im = slice(rows + base, rows + base + 16)
        cols = slice(128 * lane, 128 * lane + 128)
        tr, ti, hr, hi = tre[re, cols], tre[im, cols], hre[re, cols], hre[im, cols]
        pr, pi, cr, ci = own[re, cols], own[im, cols], cur[re, cols], cur[im, cols]
        wr, wi = pr + prv[re, cols], pi + prv[im, cols]
        ar, ai = cr + nxt[re, cols], ci + nxt[im, cols]
        yout[re, cols] = (wr * tr - wi * ti + (pr * hr - pi * hi)).astype(BF16)
        yout[im, cols] = (wr * ti + wi * tr + (pr * hi + pi * hr)).astype(BF16)
        zout[re, cols] = (ar * tr + ai * ti + (cr * hr + ci * hi)).astype(BF16)
        zout[im, cols] = (ai * tr - ar * ti + (ci * hr - cr * hi)).astype(BF16)
        cs[re, cols] = (cr * wr + ci * wi).astype(BF16)
        cs[im, cols] = (ci * wr - cr * wi).astype(BF16)

    for half in range(BLOCK // 256):
        transforms(half)
        for lane in (2 * half, 2 * half + 1):
            for base in range(0, rows, 16):
                bins(base, lane)
    acc[...] += lax.dot_general(
        cs[...], spread[...], (((1,), (1,)), ((), ())), preferred_element_type=F32
    )

    @pl.when(quarter == 128 * CPG // BLOCK - 1)
    def _():
        made = dot(t_inv3[...], stack3(acc[...]))
        share = tgrad.shape[2]
        for at in range(tgrad.shape[0]):
            tgrad[at, 0] = made[share * at : share * at + share]


def back_kernel(
    me, qf, kf, vf, g, ys, zs, sf, sb, taps, rates, resids,
    t_inv, t_ahead, t_behind, *rest,
):
    (layer, gq, gk, gv, rim, last, eq, ek, ev, coef, lg, gp) = rest[-12:]
    rows = qf.shape[0]
    lanes = range(BLOCK // 128)
    for lane in lanes:
        cols = slice(128 * lane, 128 * lane + 128)
        eight = slice(8 * lane, 8 * lane + 8)
        weight = modal_weight(rates[0, eight, :], resids[0, eight, :])
        sets = (weight * sf[lane].astype(F32), weight * sb[lane].astype(F32))
        for n, term in enumerate(chebyshev(rates[0, eight, :])):
            for at, field in enumerate(sets):
                coef[16 * at + n : 16 * at + n + 1, cols] = jnp.sum(
                    term * field, axis=0, keepdims=True
                )
    lg[...] = dot(t_inv[...], ys[...]) + dot(t_ahead[...], stack3(coef[0:16]))
    gp[...] = dot(t_inv[...], zs[...]) + dot(t_behind[...], stack3(coef[16:32]))

    for base in range(0, rows, 16):
        here = slice(base, base + 16)
        for lane in lanes:
            cols = slice(128 * lane, 128 * lane + 128)
            conv, grad = lg[here, cols], gp[here, cols]
            layer[here, cols] = (qf[here, cols].astype(F32) * conv).astype(BF16)
            eq[lane, here] = (g[here, cols].astype(F32) * conv).astype(BF16).astype(F32)
            ek[lane, here] = (grad * vf[here, cols].astype(F32)).astype(BF16).astype(F32)
            ev[lane, here] = (grad * kf[here, cols].astype(F32)).astype(BF16).astype(F32)
    for at, src in enumerate((eq, ek, ev)):
        for lane in lanes:
            cols = slice(128 * lane, 128 * lane + 128)
            src[lane, rows:] = jnp.zeros((8, 128), F32)
            rim[8 * at : 8 * at + 8, cols] = src[lane, 0:8].astype(BF16)

    def finish(r, _):
        base = pl.multiple_of(r * 32, 32)
        here = pl.ds(base, 32)
        for lane in lanes:
            cols = slice(128 * lane, 128 * lane + 128)
            for at, (src, dst) in enumerate(((eq, gq), (ek, gk), (ev, gv))):
                total = taps[7 * at : 7 * at + 1, cols] * src[lane, here, :]
                for j in range(1, 7):
                    tap = taps[7 * at + j : 7 * at + j + 1, cols]
                    total = total + tap * src[lane, pl.ds(base + j, 32), :]
                dst[here, cols] = total.astype(BF16)
                last[8 * at : 8 * at + 8, cols] = total[24:32]
        return 0

    lax.fori_loop(0, rows // 32, finish, 0)


def tail_kernel(me, last, rim, tap, gq_in, gk_in, gv_in, gq, gk, gv, ext):
    ext[:, 0:8] = jnp.zeros((3, 8, 128), F32)

    def tile(n, _):
        cols = pl.ds(pl.multiple_of(n * 128, 128), 128)
        for at, dst in enumerate((gq, gk, gv)):
            ext[at, 8:16] = rim[8 * at : 8 * at + 8, cols].astype(F32)
            total = last[8 * at : 8 * at + 8, cols]
            for j in range(1, 7):
                total = total + tap[7 * at + j : 7 * at + j + 1, cols] * ext[at, j : 8 + j]
            dst[:, cols] = total.astype(BF16)
        return 0

    lax.fori_loop(0, last.shape[1] // 128, tile, 0, unroll=4)


def shift(value, steps):
    count = lax.axis_size(AXES)
    first, last = max(0, -steps), min(count, count - steps)
    return lax.ppermute(value, AXES, [(at, at + steps) for at in range(first, last)])


def gather_own(value):
    return jnp.stack(ring_own(value))


def ring_own(value):
    count = lax.axis_size("own")
    parts = [value]
    for hop in range(1, count):
        parts.append(lax.ppermute(value, "own", [(at, (at + hop) % count) for at in range(count)]))
    return parts


def params_of(vmem):
    return pltpu.CompilerParams(
        dimension_semantics=("arbitrary",), vmem_limit_bytes=vmem
    )


def shards(query, key, value, short_taps, long_taps, decay_rate, residues, grad_out):
    rows, width = query.shape
    owners = lax.axis_size("own")
    per = width // CHUNKS
    steps = per // BLOCK
    quarters = width // owners // BLOCK
    ctx, own = lax.axis_index("ctx"), lax.axis_index("own")
    flat = ctx * owners + own
    half = width // 128
    me = jnp.stack([own, flat // half, flat % half]).astype(jnp.int32)
    table = tables(rows)
    group = BLOCK // 128
    whole = lambda shape: pl.BlockSpec(shape, lambda i, *m: (0,) * len(shape))
    edge = pl.BlockSpec((8, width), lambda i: (rows // 8 - 1, 0))

    short, poles, *rims = pl.pallas_call(
        pack_kernel,
        out_shape=(
            jax.ShapeDtypeStruct((24, 128), F32),
            jax.ShapeDtypeStruct((384, 128), F32),
        )
        + (jax.ShapeDtypeStruct((24, per), BF16),) * CHUNKS,
        grid=(1,),
        in_specs=[edge] * 3
        + [whole(short_taps.shape), whole(decay_rate.shape), whole(residues.shape), whole(long_taps.shape)],
        out_specs=(
            whole((24, 128)),
            whole((384, 128)),
        )
        + (whole((24, per)),) * CHUNKS,
        compiler_params=params_of(60 << 20),
        name="pack",
    )(query, key, value, short_taps, decay_rate, residues, long_taps)
    rims = [shift(edge_rows, 1) for edge_rows in rims]
    short_all = gather_own(short)
    poles_parts = ring_own(poles)

    def slot(me_ref, chunk):
        return (me_ref[0] - chunk + owners) % owners

    tab = lambda name: (jnp.asarray(table[name]), whole(table[name].shape))
    full = jax.ShapeDtypeStruct((rows, width), BF16)
    part = jax.ShapeDtypeStruct((rows, per), BF16)
    spectrum = jax.ShapeDtypeStruct((2 * rows, per), BF16)
    here = pl.BlockSpec((rows, BLOCK), lambda i, m: (0, i))
    bins = pl.BlockSpec((2 * rows, BLOCK), lambda i, m: (0, i))

    def wide(chunk):
        return pl.BlockSpec((rows, BLOCK), lambda i, m: (0, chunk * steps + i))

    def owned(chunk, i, me_ref):
        return slot(me_ref, chunk * (owners // CHUNKS) + i // quarters)

    def shorts(chunk):
        return pl.BlockSpec((1, 24, 128), lambda i, m: (owned(chunk, i, m), 0, 0))

    def poles_at(chunk, first):
        return pl.BlockSpec(
            (1, 8 * group, 128), lambda i, m: (owned(chunk, i, m), first + i % quarters, 0)
        )

    def call(
        kernel, cost, grid, in_specs, operands, out_shape, out_specs, scratch,
        aliases={}, after=(),
    ):
        known = 1 + len(operands)

        def body(*refs):
            kernel(*refs[:known], *refs[known + len(after) :])

        in_specs = list(in_specs) + [pl.BlockSpec(memory_space=pl.ANY)] * len(after)
        operands = list(operands) + list(after)
        return pl.pallas_call(
            body,
            out_shape=out_shape,
            grid_spec=pltpu.PrefetchScalarGridSpec(
                num_scalar_prefetch=1,
                grid=grid,
                in_specs=in_specs,
                out_specs=out_specs,
                scratch_shapes=scratch,
            ),
            input_output_aliases=aliases,
            compiler_params=params_of(60 << 20),
            cost_estimate=pl.CostEstimate(flops=cost, transcendentals=0, bytes_accessed=cost // 200),
        )(me, *operands)

    spread = jnp.asarray(table["spread"])
    spread_spec = pl.BlockSpec((128, BLOCK), lambda i, m: (0, i % quarters))

    def front(chunk, after):
        moment, moment_spec = tab("moment")
        final = chunk == CHUNKS - 1
        mom_spec = pl.BlockSpec((32, BLOCK), lambda i, m: (0, i))
        in_specs = [wide(chunk)] * 4 + [
            pl.BlockSpec((24, BLOCK), lambda i, m: (0, i)), shorts(chunk), moment_spec, spread_spec,
        ]
        operands = [query, key, value, grad_out, rims[chunk], short_all, moment, spread]
        out_shape = (part,) * 5 + (
            jax.ShapeDtypeStruct((32, per), F32), jax.ShapeDtypeStruct((24, per), F32),
        )
        out_specs = (here,) * 5 + (mom_spec, pl.BlockSpec((24, BLOCK), lambda i, m: (0, i)))
        if final:
            in_specs += [mom_spec] * chunk + [poles_at(c, 0) for c in range(CHUNKS)]
            operands += [f[5] for f in fronts] + [poles_all] * CHUNKS
            out_shape += (jax.ShapeDtypeStruct((2, CHUNKS, per // 128, 8, 128), BF16),)
            out_specs += (
                pl.BlockSpec((2, CHUNKS, group, 8, 128), lambda i, m: (0, 0, i, 0, 0)),
            )
        return call(
            functools.partial(front_kernel, pieces=CHUNKS if final else 0),
            2_000_000_000, (steps,), in_specs, operands, out_shape, out_specs,
            [pltpu.VMEM((group, rows + 8, 128), F32)] * 3,
            after=after,
        )

    fronts, behinds, aheads = [], [], []

    def exchange(chunk, after):
        prod, gconv, after = lax.optimization_barrier((fronts[chunk][3], fronts[chunk][4], after))
        behinds.append(shift(prod, 1))
        aheads.append(shift(gconv, -1))
        return after

    fronts.append(front(0, []))
    poles_all = jnp.stack(exchange(0, tuple(poles_parts)))
    for chunk in range(1, CHUNKS):
        fronts.append(front(chunk, [fronts[-1][5]]))
    states = fronts[-1][7].reshape(2 * half, 8, 128)
    arrived = lax.all_to_all(states, AXES, 0, 0, tiled=True)
    for chunk in range(1, CHUNKS):
        exchange(chunk, states)
    ctxs = lax.axis_size("ctx")
    share = rows // ctxs

    def mid(chunk, pieces, after):
        consts = [tab(name) for name in ("own", "before", "after", "taps", "head", "inverse3")]
        spec32 = pltpu.VMEM((2 * rows, BLOCK), F32)
        spec16 = pltpu.VMEM((2 * rows, BLOCK), BF16)
        return call(
            mid_kernel, 2_000_000_000, (steps,),
            [here] * 4
            + [
                poles_at(chunk, 0),
                poles_at(chunk, quarters),
                pl.BlockSpec((1, 128, 128), lambda i, m: (owned(chunk, i, m), 2, 0)),
            ]
            + [spec for _, spec in consts]
            + [spread_spec]
            + [pl.BlockSpec(memory_space=pl.ANY)] * len(pieces),
            [fronts[chunk][3], fronts[chunk][4], behinds[chunk], aheads[chunk]]
            + [poles_all] * 3
            + [c for c, _ in consts]
            + [spread]
            + pieces,
            (spectrum,) * 2 + (jax.ShapeDtypeStruct((ctxs, owners, share, 128), F32),),
            (bins,) * 2
            + (
                pl.BlockSpec(
                    (ctxs, 1, share, 128),
                    lambda i, m: (0, chunk * (owners // CHUNKS) + i // quarters, 0, 0),
                ),
            ),
            [spec16]
            + [spec32] * 6
            + [
                spec16,
                pltpu.VMEM((2 * rows, 256), BF16),
                pltpu.VMEM((2 * rows, 128), F32),
                pltpu.VMEM((16, BLOCK), F32),
            ],
            {8 + len(consts) + 1: 2} if pieces else {},
            after,
        )

    def back(chunk, ys, zs, outs, after):
        consts = [tab(name) for name in ("inverse", "ahead", "behind")]
        made = fronts[chunk]
        operands = [
            made[0], made[1], made[2], grad_out, ys, zs, carried, carried,
            made[6], poles_all, poles_all,
        ] + [c for c, _ in consts]
        in_specs = [
            here, here, here, wide(chunk), bins, bins,
            pl.BlockSpec((group, 8, 128), lambda i, m: (chunk * steps + i, 0, 0)),
            pl.BlockSpec((group, 8, 128), lambda i, m: ((CHUNKS + chunk) * steps + i, 0, 0)),
            pl.BlockSpec((24, BLOCK), lambda i, m: (0, i)),
            poles_at(chunk, 0),
            poles_at(chunk, quarters),
        ] + [spec for _, spec in consts]
        aliases = {}
        for at, out in enumerate(outs):
            aliases[1 + len(operands)] = at
            operands.append(out)
            in_specs.append(pl.BlockSpec(memory_space=pl.ANY))
        ext = pltpu.VMEM((group, rows + 8, 128), F32)
        plain = pltpu.VMEM((rows, BLOCK), F32)
        return call(
            back_kernel, 2_000_000_000, (steps,), in_specs, operands,
            (full,) * 4
            + (jax.ShapeDtypeStruct((24, per), BF16), jax.ShapeDtypeStruct((24, per), F32)),
            (wide(chunk),) * 4
            + (
                pl.BlockSpec((24, BLOCK), lambda i, m: (0, i)),
                pl.BlockSpec((24, BLOCK), lambda i, m: (0, i)),
            ),
            [ext, ext, ext, pltpu.VMEM((32, BLOCK), F32), plain, plain],
            aliases,
            after,
        )

    mids = [mid(0, [], [])]
    scanned = call(
        scan_kernel, 200_000_000, (1,),
        [
            whole(arrived.shape),
            pl.BlockSpec(
                (1, 8, 128),
                lambda i, m: (
                    (m[0] - m[2] // (half // owners) + owners) % owners, m[2] % (half // owners), 0
                ),
            ),
        ],
        (arrived, poles_all),
        jax.ShapeDtypeStruct(arrived.shape, BF16),
        whole(arrived.shape),
        [],
        after=[mids[0][2]],
    )
    carried = lax.all_to_all(scanned, AXES, 0, 0, tiled=True)

    outs, edges, lasts = (), [], []

    def finish(chunk, after):
        made = back(chunk, mids[chunk][0], mids[chunk][1], outs, after)
        edges.append(shift(made[4], -1))
        lasts.append(made[5])
        return made[:4]

    for chunk in range(1, CHUNKS):
        mids.append(mid(chunk, [mids[-1][2]], [scanned]))
    landed = lax.all_to_all(mids[-1][2].reshape(ctxs * owners, share, 128), AXES, 0, 0, tiled=True)
    for chunk in range(CHUNKS):
        outs = finish(chunk, [])
    tokens = rows * ctxs * owners
    total = landed.sum(axis=0) * (1.0 / math.sqrt(tokens * CPG))
    every = lax.all_to_all(
        jnp.broadcast_to(total[None], (ctxs, share, 128)), "ctx", 0, 0, tiled=True
    )

    every = every.reshape(rows, 128)
    grads = outs[1:4]
    for chunk in range(CHUNKS):
        grads = call(
            tail_kernel, 200_000_000, (1,),
            [whole((24, per))] * 3 + [pl.BlockSpec(memory_space=pl.ANY)] * 3,
            (lasts[chunk], edges[chunk], fronts[chunk][6], *grads),
            (full,) * 3,
            (pl.BlockSpec((8, per), lambda i, m, chunk=chunk: (rows // 8 - 1, chunk)),) * 3,
            [pltpu.VMEM((3, 16, 128), F32)],
            {4: 0, 5: 1, 6: 2},
            [every] if chunk == CHUNKS - 1 else [],
        )
    return (outs[0],) + tuple(grads) + (every,)


def solution(mesh):
    placed = (
        P(AXES, None),
        P(AXES, None),
        P(AXES, None),
        P(None, None, "own"),
        P(None, "own"),
        P(None, "own"),
        P(None, "own"),
        P(AXES, None),
    )
    return jax.shard_map(
        shards,
        mesh=mesh,
        in_specs=placed,
        out_specs=(P(AXES, None),) * 4 + (P(None, "own"),),
        check_vma=False,
    )
```
